256 devices in a mesh: frow: 8 (over y, x_lo), fcol: 32 (over z, x_hi, core).
Axes of the slice: x: 4 (x_hi: 2, x_lo: 2; x = x_hi * 2 + x_lo), y: 4, z: 8, core: 2. Of those that a mesh axis runs over, the one named last changes fastest.
Arguments:
- science: float32 [4, 1024, 4096], P(None, 'frow', 'fcol')
- pixel_mask: int32 [4, 1024, 4096], P(None, 'frow', 'fcol'), may hold values from 0 to 3, as said below
- coadd_image: float32 [1024, 4096], P('frow', 'fcol')
- coadd_variance: float32 [1024, 4096], P('frow', 'fcol'), may hold values from 0.5 to 2
- dither: int32 [4, 2], replicated, may hold values from -113 to 113, as said below
- stamps: int32 [4, 8, 32, 12], P(None, 'frow', 'fcol'), may hold values from -1 to 15, as said below
Outputs:
- scaled_difference: float32 [4, 1024, 4096], P(None, 'frow', 'fcol')
The draws below stay inside these ranges and needn't reach their ends.
Inputs may be any that keep to these rules, and one draw needn't show every extreme that they name: `pixel_mask`: 0 marks a usable pixel; 1 a bad one, 2 a saturated one, 3 both. dither[v, 0] is the row offset and dither[v, 1] the column offset of visit v. `stamps`: cell numbers, row-major over the (4) x (4) cells of the tile; distinct within a tile and visit; live entries first, then -1; at least 4 live entries, and every visit has a tile with all 12 live.
All inputs are finite; a program needn't handle non-finite values.
Results may differ from the reference program's by a relative error of at most 0.023.
Values sent between devices are 32-bit elements; how exact they have to be, the bound alone decides.
No kernel may reach another device: no remote copies, remote signals or barrier semaphores. Data moves between devices by JAX's collectives and lax.ppermute only.
A program may use at most 128 MiB of HBM per device.

```python
import math
import jax
import jax.numpy as jnp
from jax import lax

V = 4
TH = 128
TW = 128
R = 15
NB = 30
STAMP = 32
DMAX = 113
SMAX = 12
FROWS = 8
FCOLS = 32
NY = 1024
NX = 4096


def shared_fields(key):
    image_key = jax.random.fold_in(key, 11)
    offset_key = jax.random.fold_in(key, 12)
    place_key = jax.random.fold_in(key, 16)
    coadd = jnp.clip(jax.random.normal(image_key, (NY, NX), jnp.float32), -6.0, 6.0)
    offsets = jax.random.randint(offset_key, (2 * V,), -DMAX, DMAX + 1).astype(jnp.int32)
    order = jax.random.permutation(place_key, 2 * V).astype(jnp.int32)
    entry = jnp.arange(2 * V, dtype=jnp.int32)
    offsets = jnp.where(entry == order[0], jnp.int32(DMAX), offsets)
    offsets = jnp.where(entry == order[1], jnp.int32(-DMAX), offsets)
    shifts = offsets.reshape(V, 2).astype(jnp.int32)
    return (coadd, shifts)


def draw_coadd_image(key, part):
    return shared_fields(key)[0]


def draw_dither(key, part):
    return shared_fields(key)[1]


def draw_science(key, part):
    coadd, shifts = shared_fields(key)
    padded = jnp.pad(coadd, DMAX)
    shifted = jnp.stack([lax.dynamic_slice(padded, (DMAX + shifts[v, 0], DMAX + shifts[v, 1]), (NY, NX)) for v in range(V)])
    gain_key = jax.random.fold_in(key, 14)
    noise_key = jax.random.fold_in(key, 13)
    row_key = jax.random.fold_in(key, 15)
    columns = jnp.arange(NX, dtype=jnp.float32) / max(NX - 1, 1)
    row_scale = jnp.exp(jax.random.uniform(row_key, (V, NY, 1), jnp.float32, -0.6931, 0.6931))
    gains = jax.random.uniform(gain_key, (V, 1, 1), jnp.float32, 0.8, 1.2)
    noise = jnp.clip(jax.random.normal(noise_key, (V, NY, NX), jnp.float32), -6.0, 6.0)
    level = 0.3 * (1.0 + 2.0 * columns)
    return gains * shifted + level[None, None, :] * row_scale * noise


def draw_pixel_mask(key, part):
    first_key = jax.random.fold_in(key, 21)
    second_key = jax.random.fold_in(key, 22)
    flagged = (jax.random.randint(first_key, (V, NY, NX), 0, 16) == 0).astype(jnp.int32)
    saturated = (jax.random.randint(second_key, (V, NY, NX), 0, 32) == 0).astype(jnp.int32)
    return flagged + 2 * saturated


def draw_stamps(key, part):
    cell_total = TH // STAMP * (TW // STAMP)
    score_key = jax.random.fold_in(key, 31)
    count_key = jax.random.fold_in(key, 32)
    full_key = jax.random.fold_in(key, 33)
    scores = jax.random.randint(score_key, (V, FROWS, FCOLS, cell_total), 0, 65536) * cell_total
    scores = scores + jnp.arange(cell_total, dtype=jnp.int32)
    order = jnp.argsort(scores, axis=-1, stable=True)[..., :SMAX].astype(jnp.int32)
    counts = jax.random.randint(count_key, (V, FROWS, FCOLS), SMAX // 3, SMAX)
    chosen_tile = jax.random.randint(full_key, (V,), 0, FROWS * FCOLS)
    tile_number = jnp.arange(FROWS * FCOLS, dtype=jnp.int32).reshape(FROWS, FCOLS)
    counts = jnp.where(tile_number[None] == chosen_tile[:, None, None], SMAX, counts)
    slot_number = jnp.arange(SMAX, dtype=jnp.int32)
    return jnp.where(slot_number < counts[..., None], order, -1).astype(jnp.int32)


def level_of(rng, dims, split, least, top_value):
    def one(dim, parts):
        draws = jax.random.uniform(jax.random.fold_in(jax.random.fold_in(rng, 6), dim), (parts,), jnp.float32, least / len(split), top_value / len(split))
        return jnp.repeat(jnp.exp(draws), dims[dim] // parts).reshape((-1,) + (1,) * (len(dims) - dim - 1))

    factor_of = one(*split[0])
    for cut in split[1:]:
        factor_of = factor_of * one(*cut)
    return factor_of


def setup_inputs(seed: int = 0) -> dict:
    streams_of = jax.random.split(jax.random.key(seed), 7)
    return {
        "science": draw_science(jax.random.fold_in(streams_of[6], 71), 0),
        "pixel_mask": draw_pixel_mask(jax.random.fold_in(streams_of[6], 71), 0),
        "coadd_image": draw_coadd_image(jax.random.fold_in(streams_of[6], 71), 0),
        "coadd_variance": jnp.clip(jnp.exp(math.log(2.0) - 1.3862944 * jax.random.uniform(streams_of[3], (NY, NX), jnp.float32) ** level_of(streams_of[3], (NY, NX), ((0, 8), (1, 32)), -0.2, 0.2)), 0.5, 2.0),
        "dither": draw_dither(jax.random.fold_in(streams_of[6], 71), 0),
        "stamps": draw_stamps(jax.random.fold_in(streams_of[6], 71), 0),
    }


SPREADS = (0.75, 1.5, 3.0)

def kernel_table(radius):
    offsets = jnp.arange(-radius, radius + 1, dtype=jnp.float32)
    profiles = []
    for spread in SPREADS:
        for degree in range(4):
            profile = jnp.exp(-offsets * offsets / (2.0 * spread * spread)) * (offsets / spread) ** degree
            profiles.append(profile / jnp.sqrt(jnp.sum(profile * profile)))
    return jnp.stack(profiles).astype(jnp.bfloat16)

def basis_pairs():
    along_rows = []
    along_cols = []
    for family in range(3):
        for row_degree in range(4):
            for col_degree in range(4 - row_degree):
                along_rows.append(family * 4 + row_degree)
                along_cols.append(family * 4 + col_degree)
    return (along_rows, along_cols)

def solve_fit(normal_matrix, normal_vector):
    unknowns = normal_matrix.shape[-1]
    trace_sum = jnp.einsum('fii->f', normal_matrix)
    ridge_term = 0.001 * trace_sum / unknowns
    shifted = normal_matrix + ridge_term[:, None, None] * jnp.eye(unknowns, dtype=jnp.float32)
    factor = jnp.linalg.cholesky(shifted)
    solved = jax.scipy.linalg.cho_solve((factor, True), normal_vector[..., None])[..., 0]
    return solved.reshape(normal_matrix.shape[0], 3, unknowns // 3)

def reference(science, pixel_mask, coadd_image, coadd_variance, dither, stamps):
    highest = lax.Precision.HIGHEST
    table = kernel_table(R).astype(jnp.float32)
    along_rows, along_cols = basis_pairs()
    margin = DMAX + R
    padded_image = jnp.pad(coadd_image.astype(jnp.bfloat16), margin)
    padded_var = jnp.pad(coadd_variance, margin)
    col_kernels = table[:, None, None, :]
    row_kernels = table[jnp.array(along_rows)][:, None, :, None]
    cells_across = TW // STAMP
    half_rows = TH / 2.0
    half_cols = TW / 2.0
    row_coord = (jnp.arange(TH, dtype=jnp.float32) + 0.5 - half_rows) / half_rows
    col_coord = (jnp.arange(TW, dtype=jnp.float32) + 0.5 - half_cols) / half_cols
    tile_cols = jnp.arange(FCOLS, dtype=jnp.int32)

    def cut_basis(basis_images, row_begin, col_begin):
        piece = lax.dynamic_slice(basis_images, (jnp.int32(0), row_begin, col_begin), (NB, STAMP, STAMP))
        return piece.reshape(NB, STAMP * STAMP)

    def cut_plane(plane, row_begin, col_begin):
        return lax.dynamic_slice(plane, (row_begin, col_begin), (STAMP, STAMP)).reshape(STAMP * STAMP)

    def one_strip(strip_index):
        v = strip_index // FROWS
        i = strip_index % FROWS
        row_shift = dither[v, 0]
        col_shift = dither[v, 1]
        window = lax.dynamic_slice(padded_image, (i * TH + DMAX + row_shift, DMAX + col_shift), (TH + 2 * R, NX + 2 * R))
        column_pass = lax.conv_general_dilated(window.astype(jnp.float32)[None, None], col_kernels, (1, 1), 'VALID', precision=highest)[0].astype(jnp.bfloat16)
        chosen = column_pass[jnp.array(along_cols)].astype(jnp.float32)[None]
        basis_images = lax.conv_general_dilated(chosen, row_kernels, (1, 1), 'VALID', feature_group_count=NB, precision=highest)[0].astype(jnp.bfloat16)
        var_window = lax.dynamic_slice(padded_var, (i * TH + margin + row_shift, margin + col_shift), (TH, NX))
        strip_science = lax.dynamic_slice(science, (v, i * TH, jnp.int32(0)), (1, TH, NX))[0]
        strip_mask = lax.dynamic_slice(pixel_mask, (v, i * TH, jnp.int32(0)), (1, TH, NX))[0]
        usable = (strip_mask == 0).astype(jnp.float32)
        weight = usable / (0.25 + var_window)
        cell_list = stamps[v, i]
        live_slot = (cell_list >= 0).astype(jnp.float32)
        cell_index = jnp.maximum(cell_list, 0)
        cell_row = cell_index // cells_across
        cell_col = cell_index % cells_across
        row_begin = (cell_row * STAMP).astype(jnp.int32)
        col_begin = (tile_cols[:, None] * TW + cell_col * STAMP).astype(jnp.int32)
        stamp_basis = jax.vmap(jax.vmap(cut_basis, (None, 0, 0)), (None, 0, 0))(basis_images, row_begin, col_begin)
        stamp_science = jax.vmap(jax.vmap(cut_plane, (None, 0, 0)), (None, 0, 0))(strip_science, row_begin, col_begin)
        stamp_weight = jax.vmap(jax.vmap(cut_plane, (None, 0, 0)), (None, 0, 0))(weight, row_begin, col_begin)
        ones_row = jnp.ones((FCOLS, SMAX, 1, STAMP * STAMP), jnp.bfloat16)
        design = jnp.concatenate([stamp_basis, ones_row], axis=2).astype(jnp.float32)
        weighted = (design * stamp_weight[:, :, None, :]).astype(jnp.bfloat16).astype(jnp.float32)
        gram_stamp = jnp.einsum('fskp,fslp->fskl', weighted, design, precision=highest)
        right_side = jnp.einsum('fskp,fsp->fsk', weighted, stamp_science.astype(jnp.bfloat16).astype(jnp.float32), precision=highest)
        centre_row = (cell_row * STAMP + STAMP / 2.0 - half_rows) / half_rows
        centre_col = (cell_col * STAMP + STAMP / 2.0 - half_cols) / half_cols
        spatial = jnp.stack([jnp.ones_like(centre_row), centre_col, centre_row], axis=1).astype(jnp.float32)
        normal_matrix = jnp.einsum('fas,fbs,fs,fskl->fakbl', spatial, spatial, live_slot, gram_stamp, precision=highest)
        normal_matrix = normal_matrix.reshape(FCOLS, 3 * (NB + 1), 3 * (NB + 1))
        normal_vector = jnp.einsum('fas,fs,fsk->fak', spatial, live_slot, right_side, precision=highest).reshape(FCOLS, 3 * (NB + 1))
        coefficients = solve_fit(normal_matrix, normal_vector)
        basis_tiles = basis_images.astype(jnp.float32).reshape(NB, TH, FCOLS, TW)
        weighted_sums = jnp.einsum('fak,kyfx->ayfx', coefficients[:, :, :NB], basis_tiles, precision=highest)
        weighted_sums = weighted_sums + jnp.transpose(coefficients[:, :, NB])[:, None, :, None]
        fitted_model = weighted_sums[0] + col_coord[None, None, :] * weighted_sums[1] + row_coord[:, None, None] * weighted_sums[2]
        difference = strip_science - fitted_model.reshape(TH, NX)
        noise_level = jnp.sum(usable * difference * difference) / (TH * NX)
        return difference * lax.rsqrt(noise_level + var_window + 1e-06)
    strips = lax.map(one_strip, jnp.arange(V * FROWS, dtype=jnp.int32))
    return strips.reshape(V, FROWS * TH, NX)
```

```python
import functools

import jax
import jax.numpy as jnp
import numpy as np
from jax import lax
from jax.experimental import pallas as pl
from jax.experimental.pallas import tpu as pltpu
from jax.sharding import PartitionSpec as P

V = 4
TH = 128
TW = 128
R = 15
NB = 30
STAMP = 32
DMAX = 113
SMAX = 12
SPREADS = (0.75, 1.5, 3.0)
MARGIN = DMAX + R
F = 12
WROWS = 160
SLAB = 48
YB = 16
KDIM = F * SLAB + 2 * YB
PROWS = 392
BF = jnp.bfloat16
F32 = jnp.float32


def kernel_table():
    offsets = np.arange(-R, R + 1, dtype=np.float32)
    profiles = []
    for spread in SPREADS:
        for degree in range(4):
            profile = np.exp(-offsets * offsets / np.float32(2.0 * spread * spread)) * (
                offsets / np.float32(spread)
            ) ** degree
            profile = profile.astype(np.float32)
            profiles.append(profile / np.sqrt(np.sum(profile * profile)))
    return np.stack(profiles).astype(BF)


def basis_pairs():
    pairs = []
    for g in range(3):
        for a in range(4):
            for b in range(4 - a):
                pairs.append((4 * g + a, 4 * g + b))
    return pairs


def column_matrix(table):
    out = np.zeros((256, F * TW), BF)
    for f in range(F):
        for x in range(TW):
            out[x : x + 2 * R + 1, f * TW + x] = table[f]
    return out


def row_matrix(table):
    out = np.zeros((YB * 32, KDIM), BF)
    for k, (r, c) in enumerate(basis_pairs()):
        for y in range(YB):
            out[y * 32 + k, c * SLAB + y : c * SLAB + y + 2 * R + 1] = table[r]
    for y in range(YB):
        out[y * 32 + NB, F * SLAB + YB] = 1.0
        out[y * 32 + NB + 1, F * SLAB + y] = 1.0
    return out


def roll_lanes(x, shift):
    return pltpu.roll(x, shift, 1)


def body(dither, stamps, mid, left, right, science, mask, tcol, trow, diff_out, var_out, tot_out,
         planes, cbuf, sbuf, dbuf, gbuf, wbuf):
    for p in range(2):
        for b, ref in ((0, left), (1, mid), (2, right)):
            planes[p, b, 0:384, :] = ref[p]
            planes[p, b, 384:PROWS, :] = jnp.zeros((PROWS - 384, 128), F32)
    lane = lax.broadcasted_iota(jnp.int32, (8, 128), 1)
    sub = lax.broadcasted_iota(jnp.int32, (8, 128), 0)
    lane1 = lane[0:1]

    windows = []
    for v in range(V):
        dy = dither[v, 0]
        dx = dither[v, 1]
        row0 = DMAX + dy
        col0 = DMAX + dx
        b0 = lax.shift_right_logical(col0, 7)
        s = jnp.bitwise_and(col0, 127)
        back = jnp.bitwise_and(128 - s, 127)
        last = jnp.minimum(b0 + 2, 2)
        t0 = roll_lanes(planes[0, b0, pl.ds(row0, WROWS), :], back)
        t1 = roll_lanes(planes[0, b0 + 1, pl.ds(row0, WROWS), :], back)
        t2 = roll_lanes(planes[0, last, pl.ds(row0, WROWS), :], back)
        keep = lane1 < 128 - s
        windows.append(
            jnp.concatenate([jnp.where(keep, t0, t1), jnp.where(keep, t1, t2)], axis=1).astype(BF)
        )
        col1 = MARGIN + dx
        b1 = lax.shift_right_logical(col1, 7)
        s1 = jnp.bitwise_and(col1, 127)
        back1 = jnp.bitwise_and(128 - s1, 127)
        nxt = jnp.minimum(b1 + 1, 2)
        q0 = roll_lanes(planes[1, b1, pl.ds(MARGIN + dy, TH), :], back1)
        q1 = roll_lanes(planes[1, nxt, pl.ds(MARGIN + dy, TH), :], back1)
        var = jnp.where(lane1 < 128 - s1, q0, q1)
        var_out[v] = var
        usable = (mask[v] == 0).astype(F32)
        wbuf[v] = usable / (0.25 + var)
        sbuf[:, v * TW : (v + 1) * TW] = science[v].astype(BF)

    for v in range(V):
        cp = jnp.dot(windows[v], tcol[...], preferred_element_type=F32).astype(BF)
        for f in range(F):
            cbuf[f, :, v * TW : (v + 1) * TW] = cp[:, f * TW : (f + 1) * TW]

    ones_piece = jnp.ones((YB, V * TW), BF)

    def row_block(yb, carry):
        base = pl.multiple_of(yb * YB, YB)
        slab = jnp.concatenate(
            [cbuf[f, pl.ds(base, SLAB), :] for f in range(F)]
            + [sbuf[pl.ds(base, YB), :], ones_piece],
            axis=0,
        )
        out = jnp.dot(trow[...], slab, preferred_element_type=F32).astype(BF)
        dbuf[pl.ds(pl.multiple_of(yb * (YB * 32), YB * 32), YB * 32), :] = out
        return carry

    lax.fori_loop(0, TH // YB, row_block, 0)

    group_masks = [
        ((lax.broadcasted_iota(jnp.int32, (32, 128), 1) // 32) == j).astype(F32).astype(BF)
        for j in range(4)
    ]
    for v in range(V):

        def gram_row(i, carry, v=v):
            acc = jnp.zeros((32, 128), F32)
            for c in range(8):
                ws = []
                ds = [[] for _ in range(4)]
                for t in range(4):
                    y = i * 32 + c * 4 + t
                    d = dbuf[pl.ds(pl.multiple_of(y * 32, 32), 32), v * TW : (v + 1) * TW]
                    w = wbuf[v, pl.ds(y, 1), :]
                    ws.append((d.astype(F32) * w).astype(BF))
                    for j in range(4):
                        ds[j].append(d * group_masks[j])
                wcat = jnp.concatenate(ws, axis=1)
                dcat = jnp.concatenate([jnp.concatenate(q, axis=1) for q in ds], axis=0)
                acc = acc + lax.dot_general(
                    wcat, dcat, (((1,), (1,)), ((), ())), preferred_element_type=F32
                )
            gbuf[v, i] = acc
            return carry

        lax.fori_loop(0, 4, gram_row, 0)

    group = lane // 32
    xs = (group.astype(F32) - 1.5) * 0.5
    mats = []
    for v in range(V):
        use = jnp.zeros((8, 128), F32)
        cell = sub * 4 + group
        for s in range(SMAX):
            use = use + (cell == stamps[v, s]).astype(F32)
        m00 = jnp.zeros((32, 128), F32)
        m02 = jnp.zeros((32, 128), F32)
        m22 = jnp.zeros((32, 128), F32)
        for i in range(4):
            h = gbuf[v, i] * use[i : i + 1, :]
            ys = (i - 1.5) * 0.5
            m00 = m00 + h
            m02 = m02 + h * ys
            m22 = m22 + h * (ys * ys)
        x1 = xs[0:1]

        def fold(m):
            m = m + roll_lanes(m, 32)
            return m + roll_lanes(m, 64)

        m01 = fold(m00 * x1)
        m11 = fold(m00 * (x1 * x1))
        m12 = fold(m02 * x1)
        m00 = fold(m00)
        m02 = fold(m02)
        m22 = fold(m22)
        g1 = lane1 // 32
        zero = jnp.zeros((32, 128), F32)

        def block_row(a, b, c):
            return jnp.where(g1 == 0, a, jnp.where(g1 == 1, b, jnp.where(g1 == 2, c, zero)))

        mat = jnp.concatenate(
            [
                block_row(m00, m01, m02),
                block_row(m01, m11, m12),
                block_row(m02, m12, m22),
                zero,
            ],
            axis=0,
        )
        rows = lax.broadcasted_iota(jnp.int32, (128, 128), 0)
        cols = lax.broadcasted_iota(jnp.int32, (128, 128), 1)
        valid_col = (cols % 32) != 31
        mat = jnp.where(valid_col & ((rows % 32) != 31), 0.5 * (mat + mat.T), mat)
        diag = (rows == cols) & valid_col & (rows < 96)
        trace = jnp.sum(jnp.where(diag, mat, 0.0), keepdims=True)
        mat = jnp.where(diag, mat + 0.001 * trace / 93.0, mat)
        mats.append([mat[8 * r : 8 * r + 8] for r in range(12)])

    for r in range(12):
        pivots = [i for i in range(8) if (8 * r + i) % 32 != 31]
        panel = [mats[v][r] for v in range(V)]
        for i in pivots:
            p = 8 * r + i
            for v in range(V):
                cur = panel[v]
                colb = jnp.broadcast_to(cur[:, p : p + 1], (8, 128))
                rs = cur[i : i + 1, :] / colb[i : i + 1, :]
                panel[v] = jnp.where(sub == i, rs, cur - colb * rs)
        for v in range(V):
            for b in range(12):
                if b == r:
                    continue
                src = mats[v][b]
                acc = src
                for i in pivots:
                    p = 8 * r + i
                    colb = jnp.broadcast_to(src[:, p : p + 1], (8, 128))
                    acc = acc - colb * panel[v][i : i + 1, :]
                mats[v][b] = acc
            mats[v][r] = panel[v]

    row_coord = (lax.broadcasted_iota(jnp.int32, (8, 128), 0).astype(F32) + 0.5 - 64.0) / 64.0
    col_coord = (lane.astype(F32) + 0.5 - 64.0) / 64.0
    tot_rows = []
    for v in range(V):
        vec = jnp.zeros((8, 128), F32)
        for b in range(12):
            colb = jnp.broadcast_to(mats[v][b][:, 31:32], (8, 128))
            vec = vec + jnp.where(lane == sub + 8 * b, colb, 0.0)
        vec = jnp.sum(vec, axis=0, keepdims=True)
        highs = []
        lows = []
        for a in range(3):
            ca = jnp.broadcast_to(jnp.where(lane1 // 32 == a, vec, 0.0), (8, 128))
            ca = ca + roll_lanes(ca, 32)
            ca = ca + roll_lanes(ca, 64)
            ca = jnp.where(lane % 32 == 31, 0.0, ca)
            high = ca.astype(BF).astype(F32)
            low = ca - high
            for dst, val in ((highs, high), (lows, low)):
                dst.append(
                    jnp.concatenate(
                        [jnp.where(sub == lane // 32 + 4 * h, val, 0.0) for h in range(2)], axis=1
                    )
                )
        lhs = jnp.concatenate(highs + lows, axis=0).astype(BF)
        total = jnp.zeros((8, 128), F32)
        for yb in range(TH // 8):
            block = dbuf[yb * 256 : (yb + 1) * 256, v * TW : (v + 1) * TW]
            o = jnp.dot(lhs, block, preferred_element_type=F32)
            o = o[:24] + o[24:]
            model = o[0:8] + col_coord * o[8:16] + (row_coord + yb / 8.0) * o[16:24]
            rows8 = pl.ds(yb * 8, 8)
            diff = science[v, rows8, :] - model
            diff_out[v, rows8, :] = diff
            total = total + jnp.where(mask[v, rows8, :] == 0, diff * diff, 0.0)
        tot_rows.append(jnp.sum(total, axis=0, keepdims=True))
    tot_rows += [jnp.zeros((1, 128), F32)] * 4
    tot_out[...] = jnp.broadcast_to(
        jnp.sum(jnp.concatenate(tot_rows, axis=0), axis=1, keepdims=True), (8, 128)
    )


def fit_kernel(dither, stamps, mid, left, right, science, mask):
    table = kernel_table()
    vmem = pl.BlockSpec(memory_space=pltpu.VMEM)
    smem = pl.BlockSpec(memory_space=pltpu.SMEM)
    return pl.pallas_call(
        body,
        out_shape=(
            jax.ShapeDtypeStruct((V, TH, TW), F32),
            jax.ShapeDtypeStruct((V, TH, TW), F32),
            jax.ShapeDtypeStruct((8, 128), F32),
        ),
        in_specs=[smem, smem] + [vmem] * 7,
        out_specs=(vmem, vmem, vmem),
        scratch_shapes=[
            pltpu.VMEM((2, 3, PROWS, 128), F32),
            pltpu.VMEM((F, WROWS, V * TW), BF),
            pltpu.VMEM((TH, V * TW), BF),
            pltpu.VMEM((TH * 32, V * TW), BF),
            pltpu.VMEM((V, 4, 32, 128), F32),
            pltpu.VMEM((V, TH, TW), F32),
        ],
        compiler_params=pltpu.CompilerParams(vmem_limit_bytes=56 * 1024 * 1024),
        name="fit",
    )(dither, stamps, mid, left, right, science, mask,
      jnp.asarray(column_matrix(table)), jnp.asarray(row_matrix(table)))


def shift(x, axis, step):
    count = lax.axis_size(axis)
    return lax.ppermute(
        x, axis, [(i, i + step) for i in range(count) if 0 <= i + step < count]
    )


def strip_sum(x):
    for k in (1, 2, 4, 8, 16):
        x = x + lax.ppermute(x, "fcol", [(i, i ^ k) for i in range(lax.axis_size("fcol"))])
    return x


def on_device(science, pixel_mask, coadd_image, coadd_variance, dither, stamps):
    planes = jnp.stack([coadd_image, coadd_variance])
    above = shift(planes, "frow", 1)
    below = shift(planes, "frow", -1)
    mid = jnp.concatenate([above, planes, below], axis=1)
    left = shift(mid, "fcol", 1)
    right = shift(mid, "fcol", -1)
    diff, var, tot = fit_kernel(
        dither, stamps.reshape(V, SMAX), mid, left, right, science, pixel_mask
    )
    tot = strip_sum(tot)
    pixel_count = TH * TW * lax.axis_size("fcol")
    noise = tot[:V, :1].reshape(V, 1, 1) / pixel_count
    return diff * lax.rsqrt(noise + var + 1e-06)


def solution(mesh):
    in_specs = (
        P(None, "frow", "fcol"),
        P(None, "frow", "fcol"),
        P("frow", "fcol"),
        P("frow", "fcol"),
        P(),
        P(None, "frow", "fcol", None),
    )
    out_specs = P(None, "frow", "fcol")
    return jax.shard_map(
        on_device, mesh=mesh, in_specs=in_specs, out_specs=out_specs, check_vma=False
    )
```

```python
import functools

import jax
import jax.numpy as jnp
import numpy as np
from jax import lax
from jax.experimental import pallas as pl
from jax.experimental.pallas import tpu as pltpu
from jax.sharding import PartitionSpec as P

V = 4
TH = 128
TW = 128
R = 15
NB = 30
STAMP = 32
DMAX = 113
SMAX = 12
SPREADS = (0.75, 1.5, 3.0)
MARGIN = DMAX + R
F = 12
WROWS = 160
SLAB = 48
YB = 16
KDIM = F * SLAB + 2 * YB
PROWS = 392
BF = jnp.bfloat16
F32 = jnp.float32


def kernel_table():
    offsets = np.arange(-R, R + 1, dtype=np.float32)
    profiles = []
    for spread in SPREADS:
        for degree in range(4):
            profile = np.exp(-offsets * offsets / np.float32(2.0 * spread * spread)) * (
                offsets / np.float32(spread)
            ) ** degree
            profile = profile.astype(np.float32)
            profiles.append(profile / np.sqrt(np.sum(profile * profile)))
    return np.stack(profiles).astype(BF)


def basis_pairs():
    pairs = []
    for g in range(3):
        for a in range(4):
            for b in range(4 - a):
                pairs.append((4 * g + a, 4 * g + b))
    return pairs


def column_matrix(table):
    out = np.zeros((256, F * TW), BF)
    for f in range(F):
        for x in range(TW):
            out[x : x + 2 * R + 1, f * TW + x] = table[f]
    return out


def row_matrix(table):
    out = np.zeros((YB * 32, KDIM), BF)
    for k, (r, c) in enumerate(basis_pairs()):
        for y in range(YB):
            out[y * 32 + k, c * SLAB + y : c * SLAB + y + 2 * R + 1] = table[r]
    for y in range(YB):
        out[y * 32 + NB, F * SLAB + YB] = 1.0
        out[y * 32 + NB + 1, F * SLAB + y] = 1.0
    return out


def roll_lanes(x, shift):
    return pltpu.roll(x, shift, 1)


def body(dither, stamps, mid, left, right, science, mask, tcol, trow, diff_out, var_out, tot_out,
         planes, cbuf, sbuf, dbuf, gbuf, wbuf):
    for p in range(2):
        for b, ref in ((0, left), (1, mid), (2, right)):
            planes[p, b, 0:384, :] = ref[p]
            planes[p, b, 384:PROWS, :] = jnp.zeros((PROWS - 384, 128), F32)
    lane = lax.broadcasted_iota(jnp.int32, (8, 128), 1)
    sub = lax.broadcasted_iota(jnp.int32, (8, 128), 0)
    lane1 = lane[0:1]

    windows = []
    for v in range(V):
        dy = dither[v, 0]
        dx = dither[v, 1]
        row0 = DMAX + dy
        col0 = DMAX + dx
        b0 = lax.shift_right_logical(col0, 7)
        s = jnp.bitwise_and(col0, 127)
        back = jnp.bitwise_and(128 - s, 127)
        last = jnp.minimum(b0 + 2, 2)
        t0 = roll_lanes(planes[0, b0, pl.ds(row0, WROWS), :], back)
        t1 = roll_lanes(planes[0, b0 + 1, pl.ds(row0, WROWS), :], back)
        t2 = roll_lanes(planes[0, last, pl.ds(row0, WROWS), :], back)
        keep = lane1 < 128 - s
        windows.append(
            jnp.concatenate([jnp.where(keep, t0, t1), jnp.where(keep, t1, t2)], axis=1).astype(BF)
        )
        col1 = MARGIN + dx
        b1 = lax.shift_right_logical(col1, 7)
        s1 = jnp.bitwise_and(col1, 127)
        back1 = jnp.bitwise_and(128 - s1, 127)
        nxt = jnp.minimum(b1 + 1, 2)
        q0 = roll_lanes(planes[1, b1, pl.ds(MARGIN + dy, TH), :], back1)
        q1 = roll_lanes(planes[1, nxt, pl.ds(MARGIN + dy, TH), :], back1)
        var = jnp.where(lane1 < 128 - s1, q0, q1)
        var_out[v] = var
        usable = (mask[v] == 0).astype(F32)
        wbuf[v] = usable / (0.25 + var)
        sbuf[:, v * TW : (v + 1) * TW] = science[v].astype(BF)

    for v in range(V):
        cp = jnp.dot(windows[v], tcol[...], preferred_element_type=F32).astype(BF)
        for f in range(F):
            cbuf[f, :, v * TW : (v + 1) * TW] = cp[:, f * TW : (f + 1) * TW]

    ones_piece = jnp.ones((YB, V * TW), BF)

    def row_block(yb, carry):
        base = pl.multiple_of(yb * YB, YB)
        slab = jnp.concatenate(
            [cbuf[f, pl.ds(base, SLAB), :] for f in range(F)]
            + [sbuf[pl.ds(base, YB), :], ones_piece],
            axis=0,
        )
        out = jnp.dot(trow[...], slab, preferred_element_type=F32).astype(BF)
        dbuf[pl.ds(pl.multiple_of(yb * (YB * 32), YB * 32), YB * 32), :] = out
        return carry

    lax.fori_loop(0, TH // YB, row_block, 0)

    group_masks = [
        ((lax.broadcasted_iota(jnp.int32, (32, 128), 1) // 32) == j).astype(F32).astype(BF)
        for j in range(4)
    ]
    for v in range(V):

        def gram_row(i, carry, v=v):
            acc = jnp.zeros((32, 128), F32)
            for c in range(8):
                ws = []
                ds = [[] for _ in range(4)]
                for t in range(4):
                    y = i * 32 + c * 4 + t
                    d = dbuf[pl.ds(pl.multiple_of(y * 32, 32), 32), v * TW : (v + 1) * TW]
                    w = wbuf[v, pl.ds(y, 1), :]
                    ws.append((d.astype(F32) * w).astype(BF))
                    for j in range(4):
                        ds[j].append(d * group_masks[j])
                wcat = jnp.concatenate(ws, axis=1)
                dcat = jnp.concatenate([jnp.concatenate(q, axis=1) for q in ds], axis=0)
                acc = acc + lax.dot_general(
                    wcat, dcat, (((1,), (1,)), ((), ())), preferred_element_type=F32
                )
            gbuf[v, i] = acc
            return carry

        lax.fori_loop(0, 4, gram_row, 0)

    group = lane // 32
    xs = (group.astype(F32) - 1.5) * 0.5
    mats = []
    for v in range(V):
        use = jnp.zeros((8, 128), F32)
        cell = sub * 4 + group
        for s in range(SMAX):
            use = use + (cell == stamps[v, s]).astype(F32)
        m00 = jnp.zeros((32, 128), F32)
        m02 = jnp.zeros((32, 128), F32)
        m22 = jnp.zeros((32, 128), F32)
        for i in range(4):
            h = gbuf[v, i] * use[i : i + 1, :]
            ys = (i - 1.5) * 0.5
            m00 = m00 + h
            m02 = m02 + h * ys
            m22 = m22 + h * (ys * ys)
        x1 = xs[0:1]

        def fold(m):
            m = m + roll_lanes(m, 32)
            return m + roll_lanes(m, 64)

        m01 = fold(m00 * x1)
        m11 = fold(m00 * (x1 * x1))
        m12 = fold(m02 * x1)
        m00 = fold(m00)
        m02 = fold(m02)
        m22 = fold(m22)
        g1 = lane1 // 32
        zero = jnp.zeros((32, 128), F32)

        def block_row(a, b, c):
            return jnp.where(g1 == 0, a, jnp.where(g1 == 1, b, jnp.where(g1 == 2, c, zero)))

        mat = jnp.concatenate(
            [
                block_row(m00, m01, m02),
                block_row(m01, m11, m12),
                block_row(m02, m12, m22),
                zero,
            ],
            axis=0,
        )
        rows = lax.broadcasted_iota(jnp.int32, (128, 128), 0)
        cols = lax.broadcasted_iota(jnp.int32, (128, 128), 1)
        valid_col = (cols % 32) != 31
        mat = jnp.where(valid_col & ((rows % 32) != 31), 0.5 * (mat + mat.T), mat)
        diag = (rows == cols) & valid_col & (rows < 96)
        trace = jnp.sum(jnp.where(diag, mat, 0.0), keepdims=True)
        mat = jnp.where(diag, mat + 0.001 * trace / 93.0, mat)
        mats.append([mat[8 * r : 8 * r + 8] for r in range(12)])

    def lane_of(x, p):
        return jnp.broadcast_to(x[:, p : p + 1], (8, 128))

    for a in range(3):
        block = [[mats[v][4 * a + q] for q in range(4)] for v in range(V)]
        for q in range(4):
            pivots = [i for i in range(8) if 8 * q + i != 31]
            lanes = {i: 32 * a + 8 * q + i for i in pivots}
            cols = [{} for _ in range(V)]
            others = [{} for _ in range(V)]
            for i in pivots:
                for v in range(V):
                    cols[v][i] = lane_of(block[v][q], lanes[i])
            for i in pivots:
                for o in range(4):
                    if o != q:
                        for v in range(V):
                            others[v][o, i] = lane_of(block[v][o], lanes[i])
            for i in pivots:
                for v in range(V):
                    col = cols[v][i]
                    inv = 1.0 / col[i : i + 1]
                    mult = jnp.where(sub == i, -1.0, col)

                    def step(x):
                        return jnp.where(sub == i, 0.0, x) - mult * (x[i : i + 1] * inv)

                    block[v][q] = step(block[v][q])
                    for j in pivots:
                        if j > i:
                            cols[v][j] = step(cols[v][j])
            for v in range(V):
                for o in range(4):
                    if o != q:
                        acc = block[v][o]
                        for i in pivots:
                            acc = acc - others[v][o, i] * block[v][q][i : i + 1]
                        block[v][o] = acc
        rest = [r for r in range(12) if r // 4 != a]
        for v in range(V):
            for q in range(4):
                mats[v][4 * a + q] = block[v][q]
            solved = jnp.concatenate(block[v][:3] + [jnp.where(sub == 7, 0.0, block[v][3])], axis=0)
            zero = jnp.zeros((32, 128), F32)
            factor = jnp.concatenate([solved if t == a else zero for t in range(4)], axis=0)
            old = jnp.concatenate([mats[v][r] for r in rest], axis=0)
            upd = old - jnp.dot(old, factor, preferred_element_type=F32, precision=lax.Precision.HIGHEST)
            for n, r in enumerate(rest):
                mats[v][r] = upd[8 * n : 8 * n + 8]

    row_coord = (lax.broadcasted_iota(jnp.int32, (8, 128), 0).astype(F32) + 0.5 - 64.0) / 64.0
    col_coord = (lane.astype(F32) + 0.5 - 64.0) / 64.0
    tot_rows = []
    for v in range(V):
        vec = jnp.zeros((8, 128), F32)
        for b in range(12):
            colb = jnp.broadcast_to(mats[v][b][:, 31:32], (8, 128))
            vec = vec + jnp.where(lane == sub + 8 * b, colb, 0.0)
        vec = jnp.sum(vec, axis=0, keepdims=True)
        highs = []
        lows = []
        for a in range(3):
            ca = jnp.broadcast_to(jnp.where(lane1 // 32 == a, vec, 0.0), (8, 128))
            ca = ca + roll_lanes(ca, 32)
            ca = ca + roll_lanes(ca, 64)
            ca = jnp.where(lane % 32 == 31, 0.0, ca)
            high = ca.astype(BF).astype(F32)
            low = ca - high
            for dst, val in ((highs, high), (lows, low)):
                dst.append(
                    jnp.concatenate(
                        [jnp.where(sub == lane // 32 + 4 * h, val, 0.0) for h in range(2)], axis=1
                    )
                )
        lhs = jnp.concatenate(highs + lows, axis=0).astype(BF)
        total = jnp.zeros((8, 128), F32)
        for yb in range(TH // 8):
            block = dbuf[yb * 256 : (yb + 1) * 256, v * TW : (v + 1) * TW]
            o = jnp.dot(lhs, block, preferred_element_type=F32)
            o = o[:24] + o[24:]
            model = o[0:8] + col_coord * o[8:16] + (row_coord + yb / 8.0) * o[16:24]
            rows8 = pl.ds(yb * 8, 8)
            diff = science[v, rows8, :] - model
            diff_out[v, rows8, :] = diff
            total = total + jnp.where(mask[v, rows8, :] == 0, diff * diff, 0.0)
        tot_rows.append(jnp.sum(total, axis=0, keepdims=True))
    tot_rows += [jnp.zeros((1, 128), F32)] * 4
    tot_out[...] = jnp.broadcast_to(
        jnp.sum(jnp.concatenate(tot_rows, axis=0), axis=1, keepdims=True), (8, 128)
    )


def fit_kernel(dither, stamps, mid, left, right, science, mask):
    table = kernel_table()
    vmem = pl.BlockSpec(memory_space=pltpu.VMEM)
    smem = pl.BlockSpec(memory_space=pltpu.SMEM)
    return pl.pallas_call(
        body,
        out_shape=(
            jax.ShapeDtypeStruct((V, TH, TW), F32),
            jax.ShapeDtypeStruct((V, TH, TW), F32),
            jax.ShapeDtypeStruct((8, 128), F32),
        ),
        in_specs=[smem, smem] + [vmem] * 7,
        out_specs=(vmem, vmem, vmem),
        scratch_shapes=[
            pltpu.VMEM((2, 3, PROWS, 128), F32),
            pltpu.VMEM((F, WROWS, V * TW), BF),
            pltpu.VMEM((TH, V * TW), BF),
            pltpu.VMEM((TH * 32, V * TW), BF),
            pltpu.VMEM((V, 4, 32, 128), F32),
            pltpu.VMEM((V, TH, TW), F32),
        ],
        compiler_params=pltpu.CompilerParams(vmem_limit_bytes=20 * 1024 * 1024),
        name="fit",
    )(dither, stamps, mid, left, right, science, mask,
      jnp.asarray(column_matrix(table)), jnp.asarray(row_matrix(table)))


def shift(x, axis, step):
    count = lax.axis_size(axis)
    return lax.ppermute(
        x, axis, [(i, i + step) for i in range(count) if 0 <= i + step < count]
    )


def strip_sum(x):
    for k in (1, 2, 4, 8, 16):
        x = x + lax.ppermute(x, "fcol", [(i, i ^ k) for i in range(lax.axis_size("fcol"))])
    return x


def on_device(science, pixel_mask, coadd_image, coadd_variance, dither, stamps):
    planes = jnp.stack([coadd_image, coadd_variance])
    above = shift(planes, "frow", 1)
    below = shift(planes, "frow", -1)
    mid = jnp.concatenate([above, planes, below], axis=1)
    left = shift(mid, "fcol", 1)
    right = shift(mid, "fcol", -1)
    diff, var, tot = fit_kernel(
        dither, stamps.reshape(V, SMAX), mid, left, right, science, pixel_mask
    )
    tot = strip_sum(tot)
    pixel_count = TH * TW * lax.axis_size("fcol")
    noise = tot[:V, :1].reshape(V, 1, 1) / pixel_count
    return diff * lax.rsqrt(noise + var + 1e-06)


def solution(mesh):
    in_specs = (
        P(None, "frow", "fcol"),
        P(None, "frow", "fcol"),
        P("frow", "fcol"),
        P("frow", "fcol"),
        P(),
        P(None, "frow", "fcol", None),
    )
    out_specs = P(None, "frow", "fcol")
    return jax.shard_map(
        on_device, mesh=mesh, in_specs=in_specs, out_specs=out_specs, check_vma=False
    )
```

```python
import functools

import jax
import jax.numpy as jnp
import numpy as np
from jax import lax
from jax.experimental import pallas as pl
from jax.experimental.pallas import tpu as pltpu
from jax.sharding import PartitionSpec as P

V = 4
TH = 128
TW = 128
R = 15
NB = 30
STAMP = 32
DMAX = 113
SMAX = 12
SPREADS = (0.75, 1.5, 3.0)
MARGIN = DMAX + R
F = 12
WROWS = 160
SLAB = 48
YB = 16
KDIM = F * SLAB + 2 * YB
PROWS = 392
BF = jnp.bfloat16
F32 = jnp.float32


def kernel_table():
    offsets = np.arange(-R, R + 1, dtype=np.float32)
    profiles = []
    for spread in SPREADS:
        for degree in range(4):
            profile = np.exp(-offsets * offsets / np.float32(2.0 * spread * spread)) * (
                offsets / np.float32(spread)
            ) ** degree
            profile = profile.astype(np.float32)
            profiles.append(profile / np.sqrt(np.sum(profile * profile)))
    return np.stack(profiles).astype(BF)


def basis_pairs():
    pairs = []
    for g in range(3):
        for a in range(4):
            for b in range(4 - a):
                pairs.append((4 * g + a, 4 * g + b))
    return pairs


def column_matrix(table):
    out = np.zeros((256, F * TW), BF)
    for f in range(F):
        for x in range(TW):
            out[x : x + 2 * R + 1, f * TW + x] = table[f]
    return out


def row_matrix(table):
    out = np.zeros((YB * 32, KDIM), BF)
    for k, (r, c) in enumerate(basis_pairs()):
        for y in range(YB):
            out[y * 32 + k, c * SLAB + y : c * SLAB + y + 2 * R + 1] = table[r]
    for y in range(YB):
        out[y * 32 + NB, F * SLAB + YB] = 1.0
        out[y * 32 + NB + 1, F * SLAB + y] = 1.0
    return out


def roll_lanes(x, shift):
    return pltpu.roll(x, shift, 1)


def body(dither, stamps, parity, mid, side_a, side_b, visits, tables,
         diff_out, var_out, tot_out, planes, cbuf, sbuf, dbuf, gbuf, wbuf):
    row_a = pl.multiple_of(parity[0] * 256, 128)
    row_b = pl.multiple_of(256 - parity[0] * 256, 128)
    for p in range(2):
        for b, ref in ((1, mid), (2 * parity[1], side_a), (2 - 2 * parity[1], side_b)):
            planes[p, b, pl.ds(row_a, 128), :] = ref[p, 0:128, :]
            planes[p, b, 128:256, :] = ref[p, 128:256, :]
            planes[p, b, pl.ds(row_b, 128), :] = ref[p, 256:384, :]
            planes[p, b, 384:PROWS, :] = jnp.zeros((PROWS - 384, 128), F32)
    lane = lax.broadcasted_iota(jnp.int32, (8, 128), 1)
    sub = lax.broadcasted_iota(jnp.int32, (8, 128), 0)
    lane1 = lane[0:1]

    windows = []
    for v in range(V):
        dy = dither[v, 0]
        dx = dither[v, 1]
        row0 = DMAX + dy
        col0 = DMAX + dx
        b0 = lax.shift_right_logical(col0, 7)
        s = jnp.bitwise_and(col0, 127)
        back = jnp.bitwise_and(128 - s, 127)
        last = jnp.minimum(b0 + 2, 2)
        t0 = roll_lanes(planes[0, b0, pl.ds(row0, WROWS), :], back)
        t1 = roll_lanes(planes[0, b0 + 1, pl.ds(row0, WROWS), :], back)
        t2 = roll_lanes(planes[0, last, pl.ds(row0, WROWS), :], back)
        keep = lane1 < 128 - s
        windows.append(
            jnp.concatenate([jnp.where(keep, t0, t1), jnp.where(keep, t1, t2)], axis=1).astype(BF)
        )
        col1 = MARGIN + dx
        b1 = lax.shift_right_logical(col1, 7)
        s1 = jnp.bitwise_and(col1, 127)
        back1 = jnp.bitwise_and(128 - s1, 127)
        nxt = jnp.minimum(b1 + 1, 2)
        q0 = roll_lanes(planes[1, b1, pl.ds(MARGIN + dy, TH), :], back1)
        q1 = roll_lanes(planes[1, nxt, pl.ds(MARGIN + dy, TH), :], back1)
        var = jnp.where(lane1 < 128 - s1, q0, q1)
        var_out[v] = var
        wbuf[v] = visits[V + v] / (0.25 + var)
        sbuf[:, v * TW : (v + 1) * TW] = visits[v].astype(BF)

    for v in range(V):
        cp = jnp.dot(windows[v], tables[0:256, :], preferred_element_type=F32).astype(BF)
        for f in range(F):
            cbuf[f, :, v * TW : (v + 1) * TW] = cp[:, f * TW : (f + 1) * TW]

    ones_piece = jnp.ones((YB, V * TW), BF)

    def row_block(yb, carry):
        base = pl.multiple_of(yb * YB, YB)
        slab = jnp.concatenate(
            [cbuf[f, pl.ds(base, SLAB), :] for f in range(F)]
            + [sbuf[pl.ds(base, YB), :], ones_piece],
            axis=0,
        )
        trow = jnp.concatenate([tables[256:512, 0:KDIM], tables[256:512, 640 : 640 + KDIM]], axis=0)
        out = jnp.dot(trow, slab, preferred_element_type=F32).astype(BF)
        dbuf[pl.ds(pl.multiple_of(yb * (YB * 32), YB * 32), YB * 32), :] = out
        return carry

    lax.fori_loop(0, TH // YB, row_block, 0)

    lanes32 = lax.broadcasted_iota(jnp.int32, (32, 128), 1)
    half_masks = [(lanes32 // 64 == h).astype(F32) for h in range(2)]
    odd_masks = [((lanes32 // 32) % 2 == h).astype(F32).astype(BF) for h in range(2)]
    for v in range(V):

        def gram_row(i, carry, v=v):
            acc = jnp.zeros((64, 64), F32)
            for c in range(8):
                ws = []
                ds = []
                for t in range(4):
                    y = i * 32 + c * 4 + t
                    d = dbuf[pl.ds(pl.multiple_of(y * 32, 32), 32), v * TW : (v + 1) * TW]
                    w = d.astype(F32) * wbuf[v, pl.ds(y, 1), :]
                    ws.append(jnp.concatenate([(w * m).astype(BF) for m in half_masks], axis=0))
                    ds.append(jnp.concatenate([d * m for m in odd_masks], axis=0))
                acc = acc + lax.dot_general(
                    jnp.concatenate(ws, axis=1),
                    jnp.concatenate(ds, axis=1),
                    (((1,), (1,)), ((), ())),
                    preferred_element_type=F32,
                )
            gbuf[v, i] = jnp.concatenate([acc[:32], acc[32:]], axis=1)
            return carry

        lax.fori_loop(0, 4, gram_row, 0)

    group = lane // 32
    xs = (group.astype(F32) - 1.5) * 0.5
    mats = []
    for v in range(V):
        use = jnp.zeros((8, 128), F32)
        cell = sub * 4 + group
        for s in range(SMAX):
            use = use + (cell == stamps[v, s]).astype(F32)
        m00 = jnp.zeros((32, 128), F32)
        m02 = jnp.zeros((32, 128), F32)
        m22 = jnp.zeros((32, 128), F32)
        for i in range(4):
            h = gbuf[v, i] * use[i : i + 1, :]
            ys = (i - 1.5) * 0.5
            m00 = m00 + h
            m02 = m02 + h * ys
            m22 = m22 + h * (ys * ys)
        x1 = xs[0:1]

        def fold(m):
            m = m + roll_lanes(m, 32)
            return m + roll_lanes(m, 64)

        m01 = fold(m00 * x1)
        m11 = fold(m00 * (x1 * x1))
        m12 = fold(m02 * x1)
        m00 = fold(m00)
        m02 = fold(m02)
        m22 = fold(m22)
        g1 = lane1 // 32
        zero = jnp.zeros((32, 128), F32)

        def block_row(a, b, c):
            return jnp.where(g1 == 0, a, jnp.where(g1 == 1, b, jnp.where(g1 == 2, c, zero)))

        mat = jnp.concatenate(
            [
                block_row(m00, m01, m02),
                block_row(m01, m11, m12),
                block_row(m02, m12, m22),
                zero,
            ],
            axis=0,
        )
        rows = lax.broadcasted_iota(jnp.int32, (128, 128), 0)
        cols = lax.broadcasted_iota(jnp.int32, (128, 128), 1)
        valid_col = (cols % 32) != 31
        mat = jnp.where(valid_col & ((rows % 32) != 31), 0.5 * (mat + mat.T), mat)
        diag = (rows == cols) & valid_col & (rows < 96)
        trace = jnp.sum(jnp.where(diag, mat, 0.0), keepdims=True)
        mat = jnp.where(diag, mat + 0.001 * trace / 93.0, mat)
        mats.append([mat[8 * r : 8 * r + 8] for r in range(12)])

    def lane_of(x, p):
        return jnp.broadcast_to(x[:, p : p + 1], (8, 128))

    for a in range(3):
        block = [[mats[v][4 * a + q] for q in range(4)] for v in range(V)]
        for q in range(4):
            pivots = [i for i in range(8) if 8 * q + i != 31]
            lanes = {i: 32 * a + 8 * q + i for i in pivots}
            cols = [{} for _ in range(V)]
            others = [{} for _ in range(V)]
            for i in pivots:
                for v in range(V):
                    cols[v][i] = lane_of(block[v][q], lanes[i])
            for i in pivots:
                for o in range(4):
                    if o != q:
                        for v in range(V):
                            others[v][o, i] = lane_of(block[v][o], lanes[i])
            for i in pivots:
                for v in range(V):
                    col = cols[v][i]
                    inv = 1.0 / col[i : i + 1]
                    mult = jnp.where(sub == i, -1.0, col)

                    def step(x):
                        return jnp.where(sub == i, 0.0, x) - mult * (x[i : i + 1] * inv)

                    block[v][q] = step(block[v][q])
                    for j in pivots:
                        if j > i:
                            cols[v][j] = step(cols[v][j])
            for v in range(V):
                for o in range(4):
                    if o != q:
                        acc = block[v][o]
                        for i in pivots:
                            acc = acc - others[v][o, i] * block[v][q][i : i + 1]
                        block[v][o] = acc
        rest = [r for r in range(12) if r // 4 != a]
        for v in range(V):
            for q in range(4):
                mats[v][4 * a + q] = block[v][q]
            solved = jnp.concatenate(block[v][:3] + [jnp.where(sub == 7, 0.0, block[v][3])], axis=0)
            zero = jnp.zeros((32, 128), F32)
            factor = jnp.concatenate([solved if t == a else zero for t in range(4)], axis=0)
            old = jnp.concatenate([mats[v][r] for r in rest], axis=0)
            upd = old - jnp.dot(old, factor, preferred_element_type=F32, precision=lax.Precision.HIGHEST)
            for n, r in enumerate(rest):
                mats[v][r] = upd[8 * n : 8 * n + 8]

    row_coord = (lax.broadcasted_iota(jnp.int32, (8, 128), 0).astype(F32) + 0.5 - 64.0) / 64.0
    col_coord = (lane.astype(F32) + 0.5 - 64.0) / 64.0
    tot_rows = []
    for v in range(V):
        vec = jnp.zeros((8, 128), F32)
        for b in range(12):
            colb = jnp.broadcast_to(mats[v][b][:, 31:32], (8, 128))
            vec = vec + jnp.where(lane == sub + 8 * b, colb, 0.0)
        vec = jnp.sum(vec, axis=0, keepdims=True)
        highs = []
        lows = []
        for a in range(3):
            ca = jnp.broadcast_to(jnp.where(lane1 // 32 == a, vec, 0.0), (8, 128))
            ca = ca + roll_lanes(ca, 32)
            ca = ca + roll_lanes(ca, 64)
            ca = jnp.where(lane % 32 == 31, 0.0, ca)
            high = ca.astype(BF).astype(F32)
            low = ca - high
            for dst, val in ((highs, high), (lows, low)):
                dst.append(
                    jnp.concatenate(
                        [jnp.where(sub == lane // 32 + 4 * h, val, 0.0) for h in range(2)], axis=1
                    )
                )
        lhs = jnp.concatenate(highs + lows, axis=0).astype(BF)
        total = jnp.zeros((8, 128), F32)
        for yb in range(TH // 8):
            block = dbuf[yb * 256 : (yb + 1) * 256, v * TW : (v + 1) * TW]
            o = jnp.dot(lhs, block, preferred_element_type=F32)
            o = o[:24] + o[24:]
            model = o[0:8] + col_coord * o[8:16] + (row_coord + yb / 8.0) * o[16:24]
            rows8 = pl.ds(yb * 8, 8)
            diff = visits[v, rows8, :] - model
            diff_out[v, rows8, :] = diff
            total = total + visits[V + v, rows8, :] * (diff * diff)
        tot_rows.append(jnp.sum(total, axis=0, keepdims=True))
    tot_rows += [jnp.zeros((1, 128), F32)] * 4
    tot_out[...] = jnp.broadcast_to(
        jnp.sum(jnp.concatenate(tot_rows, axis=0), axis=1, keepdims=True), (8, 128)
    )


def fit_kernel(dither, stamps, parity, mid, side_a, side_b, visits):
    table = kernel_table()
    vmem = pl.BlockSpec(memory_space=pltpu.VMEM)
    smem = pl.BlockSpec(memory_space=pltpu.SMEM)
    tables = np.zeros((512, F * TW), BF)
    tables[0:256] = column_matrix(table)
    rows = row_matrix(table)
    tables[256:512, 0:KDIM] = rows[0:256]
    tables[256:512, 640 : 640 + KDIM] = rows[256:512]
    return pl.pallas_call(
        body,
        out_shape=(
            jax.ShapeDtypeStruct((V, TH, TW), F32),
            jax.ShapeDtypeStruct((V, TH, TW), F32),
            jax.ShapeDtypeStruct((8, 128), F32),
        ),
        in_specs=[smem] * 3 + [vmem] * 5,
        out_specs=(vmem, vmem, vmem),
        scratch_shapes=[
            pltpu.VMEM((2, 3, PROWS, 128), F32),
            pltpu.VMEM((F, WROWS, V * TW), BF),
            pltpu.VMEM((TH, V * TW), BF),
            pltpu.VMEM((TH * 32, V * TW), BF),
            pltpu.VMEM((V, 4, 32, 128), F32),
            pltpu.VMEM((V, TH, TW), F32),
        ],
        compiler_params=pltpu.CompilerParams(vmem_limit_bytes=20 * 1024 * 1024),
        name="fit",
    )(dither, stamps, parity, mid, side_a, side_b, visits, jnp.asarray(tables))


def exchange(x, axis, first):
    pairs = []
    for i in range(first, lax.axis_size(axis) - 1, 2):
        pairs += [(i, i + 1), (i + 1, i)]
    return lax.ppermute(x, axis, pairs)


def strip_sum(x):
    count = lax.axis_size("fcol")
    parts = jnp.broadcast_to(x[None, :], (count, x.shape[0]))
    return jnp.sum(lax.all_to_all(parts, "fcol", 0, 0, tiled=True), axis=0)


def on_device(science, pixel_mask, coadd_image, coadd_variance, dither, stamps):
    parity = jnp.bitwise_and(jnp.stack([lax.axis_index("frow"), lax.axis_index("fcol")]), 1)
    planes = lax.optimization_barrier(jnp.stack([coadd_image, coadd_variance]))
    rows_a = exchange(planes, "frow", 1)
    rows_b = exchange(planes, "frow", 0)
    mid = jnp.concatenate([rows_a, planes, rows_b], axis=1)
    mid, science, pixel_mask = lax.optimization_barrier((mid, science, pixel_mask))
    visits = jnp.concatenate([science, (pixel_mask == 0).astype(F32)], axis=0)
    side_b = exchange(mid, "fcol", 0)
    side_a = exchange(mid, "fcol", 1)
    diff, var, tot = fit_kernel(
        dither, stamps.reshape(V, SMAX), parity, mid, side_a, side_b, visits
    )
    tot = strip_sum(tot[:V, 0])
    pixel_count = TH * TW * lax.axis_size("fcol")
    noise = tot.reshape(V, 1, 1) / pixel_count
    return diff * lax.rsqrt(noise + var + 1e-06)


def solution(mesh):
    in_specs = (
        P(None, "frow", "fcol"),
        P(None, "frow", "fcol"),
        P("frow", "fcol"),
        P("frow", "fcol"),
        P(),
        P(None, "frow", "fcol", None),
    )
    out_specs = P(None, "frow", "fcol")
    return jax.shard_map(
        on_device, mesh=mesh, in_specs=in_specs, out_specs=out_specs, check_vma=False
    )
```

```python
import functools

import jax
import jax.numpy as jnp
import numpy as np
from jax import lax
from jax.experimental import pallas as pl
from jax.experimental.pallas import tpu as pltpu
from jax.sharding import PartitionSpec as P

V = 4
TH = 128
TW = 128
R = 15
NB = 30
STAMP = 32
DMAX = 113
SMAX = 12
SPREADS = (0.75, 1.5, 3.0)
MARGIN = DMAX + R
F = 12
WROWS = 160
SLAB = 48
YB = 16
KDIM = F * SLAB + 2 * YB
PROWS = 392
BF = jnp.bfloat16
F32 = jnp.float32


def kernel_table():
    offsets = np.arange(-R, R + 1, dtype=np.float32)
    profiles = []
    for spread in SPREADS:
        for degree in range(4):
            profile = np.exp(-offsets * offsets / np.float32(2.0 * spread * spread)) * (
                offsets / np.float32(spread)
            ) ** degree
            profile = profile.astype(np.float32)
            profiles.append(profile / np.sqrt(np.sum(profile * profile)))
    return np.stack(profiles).astype(BF)


def basis_pairs():
    pairs = []
    for g in range(3):
        for a in range(4):
            for b in range(4 - a):
                pairs.append((4 * g + a, 4 * g + b))
    return pairs


def column_matrix(table):
    out = np.zeros((256, F * TW), BF)
    for f in range(F):
        for x in range(TW):
            out[x : x + 2 * R + 1, f * TW + x] = table[f]
    return out


def row_matrix(table):
    out = np.zeros((YB * 32, KDIM), BF)
    for k, (r, c) in enumerate(basis_pairs()):
        for y in range(YB):
            out[y * 32 + k, c * SLAB + y : c * SLAB + y + 2 * R + 1] = table[r]
    for y in range(YB):
        out[y * 32 + NB, F * SLAB + YB] = 1.0
        out[y * 32 + NB + 1, F * SLAB + y] = 1.0
    return out


def roll_lanes(x, shift):
    return pltpu.roll(x, shift, 1)


def gather_planes(planes, parity, mid, side_a, side_b):
    row_a = pl.multiple_of(parity[0] * 256, 128)
    row_b = pl.multiple_of(256 - parity[0] * 256, 128)
    for b, ref in ((1, mid), (2 * parity[1], side_a), (2 - 2 * parity[1], side_b)):
        planes[b, pl.ds(row_a, 128), :] = ref[0:128, :]
        planes[b, 128:256, :] = ref[128:256, :]
        planes[b, pl.ds(row_b, 128), :] = ref[256:384, :]
        planes[b, 384:PROWS, :] = jnp.zeros((PROWS - 384, 128), F32)


def basis_body(dither, parity, mid, side_a, side_b, visits, tables, dbuf, planes, cbuf, sbuf):
    gather_planes(planes, parity, mid.at[0], side_a, side_b.at[0])
    lane1 = lax.broadcasted_iota(jnp.int32, (1, 128), 1)
    windows = []
    for v in range(V):
        row0 = DMAX + dither[v, 0]
        col0 = DMAX + dither[v, 1]
        b0 = lax.shift_right_logical(col0, 7)
        s = jnp.bitwise_and(col0, 127)
        back = jnp.bitwise_and(128 - s, 127)
        last = jnp.minimum(b0 + 2, 2)
        t0 = roll_lanes(planes[b0, pl.ds(row0, WROWS), :], back)
        t1 = roll_lanes(planes[b0 + 1, pl.ds(row0, WROWS), :], back)
        t2 = roll_lanes(planes[last, pl.ds(row0, WROWS), :], back)
        keep = lane1 < 128 - s
        windows.append(
            jnp.concatenate([jnp.where(keep, t0, t1), jnp.where(keep, t1, t2)], axis=1).astype(BF)
        )
        sbuf[:, v * TW : (v + 1) * TW] = visits[v].astype(BF)

    for v in range(V):
        cp = jnp.dot(windows[v], tables[0:256, :], preferred_element_type=F32).astype(BF)
        for f in range(F):
            cbuf[f, :, v * TW : (v + 1) * TW] = cp[:, f * TW : (f + 1) * TW]

    ones_piece = jnp.ones((YB, V * TW), BF)

    def row_block(yb, carry):
        base = pl.multiple_of(yb * YB, YB)
        slab = jnp.concatenate(
            [cbuf[f, pl.ds(base, SLAB), :] for f in range(F)]
            + [sbuf[pl.ds(base, YB), :], ones_piece],
            axis=0,
        )
        trow = jnp.concatenate([tables[256:512, 0:KDIM], tables[256:512, 640 : 640 + KDIM]], axis=0)
        out = jnp.dot(trow, slab, preferred_element_type=F32).astype(BF)
        dbuf[pl.ds(pl.multiple_of(yb * (YB * 32), YB * 32), YB * 32), :] = out
        return carry

    lax.fori_loop(0, TH // YB, row_block, 0)


def fit_body(dither, stamps, parity, mid, side_a, side_b, visits, dbuf,
             diff_out, var_out, tot_out, planes, gbuf, wbuf):
    gather_planes(planes, parity, mid.at[1], side_a, side_b.at[1])
    lane = lax.broadcasted_iota(jnp.int32, (8, 128), 1)
    sub = lax.broadcasted_iota(jnp.int32, (8, 128), 0)
    lane1 = lane[0:1]
    for v in range(V):
        row1 = MARGIN + dither[v, 0]
        col1 = MARGIN + dither[v, 1]
        b1 = lax.shift_right_logical(col1, 7)
        s1 = jnp.bitwise_and(col1, 127)
        back1 = jnp.bitwise_and(128 - s1, 127)
        nxt = jnp.minimum(b1 + 1, 2)
        q0 = roll_lanes(planes[b1, pl.ds(row1, TH), :], back1)
        q1 = roll_lanes(planes[nxt, pl.ds(row1, TH), :], back1)
        var = jnp.where(lane1 < 128 - s1, q0, q1)
        var_out[v] = var
        wbuf[v] = visits[V + v] / (0.25 + var)

    lanes32 = lax.broadcasted_iota(jnp.int32, (32, 128), 1)
    half_masks = [(lanes32 // 64 == h).astype(F32) for h in range(2)]
    odd_masks = [((lanes32 // 32) % 2 == h).astype(F32).astype(BF) for h in range(2)]
    for v in range(V):

        def gram_row(i, carry, v=v):
            acc = jnp.zeros((64, 64), F32)
            for c in range(8):
                ws = []
                ds = []
                for t in range(4):
                    y = i * 32 + c * 4 + t
                    d = dbuf[pl.ds(pl.multiple_of(y * 32, 32), 32), v * TW : (v + 1) * TW]
                    w = d.astype(F32) * wbuf[v, pl.ds(y, 1), :]
                    ws.append(jnp.concatenate([(w * m).astype(BF) for m in half_masks], axis=0))
                    ds.append(jnp.concatenate([d * m for m in odd_masks], axis=0))
                acc = acc + lax.dot_general(
                    jnp.concatenate(ws, axis=1),
                    jnp.concatenate(ds, axis=1),
                    (((1,), (1,)), ((), ())),
                    preferred_element_type=F32,
                )
            gbuf[v, i] = jnp.concatenate([acc[:32], acc[32:]], axis=1)
            return carry

        lax.fori_loop(0, 4, gram_row, 0)

    group = lane // 32
    xs = (group.astype(F32) - 1.5) * 0.5
    mats = []
    for v in range(V):
        use = jnp.zeros((8, 128), F32)
        cell = sub * 4 + group
        for s in range(SMAX):
            use = use + (cell == stamps[v, s]).astype(F32)
        m00 = jnp.zeros((32, 128), F32)
        m02 = jnp.zeros((32, 128), F32)
        m22 = jnp.zeros((32, 128), F32)
        for i in range(4):
            h = gbuf[v, i] * use[i : i + 1, :]
            ys = (i - 1.5) * 0.5
            m00 = m00 + h
            m02 = m02 + h * ys
            m22 = m22 + h * (ys * ys)
        x1 = xs[0:1]

        def fold(m):
            m = m + roll_lanes(m, 32)
            return m + roll_lanes(m, 64)

        m01 = fold(m00 * x1)
        m11 = fold(m00 * (x1 * x1))
        m12 = fold(m02 * x1)
        m00 = fold(m00)
        m02 = fold(m02)
        m22 = fold(m22)
        g1 = lane1 // 32
        zero = jnp.zeros((32, 128), F32)

        def block_row(a, b, c):
            return jnp.where(g1 == 0, a, jnp.where(g1 == 1, b, jnp.where(g1 == 2, c, zero)))

        mat = jnp.concatenate(
            [
                block_row(m00, m01, m02),
                block_row(m01, m11, m12),
                block_row(m02, m12, m22),
                zero,
            ],
            axis=0,
        )
        rows = lax.broadcasted_iota(jnp.int32, (128, 128), 0)
        cols = lax.broadcasted_iota(jnp.int32, (128, 128), 1)
        valid_col = (cols % 32) != 31
        mat = jnp.where(valid_col & ((rows % 32) != 31), 0.5 * (mat + mat.T), mat)
        diag = (rows == cols) & valid_col & (rows < 96)
        trace = jnp.sum(jnp.where(diag, mat, 0.0), keepdims=True)
        mat = jnp.where(diag, mat + 0.001 * trace / 93.0, mat)
        mats.append([mat[8 * r : 8 * r + 8] for r in range(12)])

    def lane_of(x, p):
        return jnp.broadcast_to(x[:, p : p + 1], (8, 128))

    for a in range(3):
        block = [[mats[v][4 * a + q] for q in range(4)] for v in range(V)]
        for q in range(4):
            pivots = [i for i in range(8) if 8 * q + i != 31]
            lanes = {i: 32 * a + 8 * q + i for i in pivots}
            cols = [{} for _ in range(V)]
            others = [{} for _ in range(V)]
            for i in pivots:
                for v in range(V):
                    cols[v][i] = lane_of(block[v][q], lanes[i])
            for i in pivots:
                for o in range(4):
                    if o != q:
                        for v in range(V):
                            others[v][o, i] = lane_of(block[v][o], lanes[i])
            for i in pivots:
                for v in range(V):
                    col = cols[v][i]
                    inv = 1.0 / col[i : i + 1]
                    mult = jnp.where(sub == i, -1.0, col)

                    def step(x):
                        return jnp.where(sub == i, 0.0, x) - mult * (x[i : i + 1] * inv)

                    block[v][q] = step(block[v][q])
                    for j in pivots:
                        if j > i:
                            cols[v][j] = step(cols[v][j])
            for v in range(V):
                for o in range(4):
                    if o != q:
                        acc = block[v][o]
                        for i in pivots:
                            acc = acc - others[v][o, i] * block[v][q][i : i + 1]
                        block[v][o] = acc
        rest = [r for r in range(12) if r // 4 != a]
        for v in range(V):
            for q in range(4):
                mats[v][4 * a + q] = block[v][q]
            solved = jnp.concatenate(block[v][:3] + [jnp.where(sub == 7, 0.0, block[v][3])], axis=0)
            zero = jnp.zeros((32, 128), F32)
            factor = jnp.concatenate([solved if t == a else zero for t in range(4)], axis=0)
            old = jnp.concatenate([mats[v][r] for r in rest], axis=0)
            upd = old - jnp.dot(old, factor, preferred_element_type=F32, precision=lax.Precision.HIGHEST)
            for n, r in enumerate(rest):
                mats[v][r] = upd[8 * n : 8 * n + 8]

    row_coord = (lax.broadcasted_iota(jnp.int32, (8, 128), 0).astype(F32) + 0.5 - 64.0) / 64.0
    col_coord = (lane.astype(F32) + 0.5 - 64.0) / 64.0
    tot_rows = []
    for v in range(V):
        vec = jnp.zeros((8, 128), F32)
        for b in range(12):
            colb = jnp.broadcast_to(mats[v][b][:, 31:32], (8, 128))
            vec = vec + jnp.where(lane == sub + 8 * b, colb, 0.0)
        vec = jnp.sum(vec, axis=0, keepdims=True)
        highs = []
        lows = []
        for a in range(3):
            ca = jnp.broadcast_to(jnp.where(lane1 // 32 == a, vec, 0.0), (8, 128))
            ca = ca + roll_lanes(ca, 32)
            ca = ca + roll_lanes(ca, 64)
            ca = jnp.where(lane % 32 == 31, 0.0, ca)
            high = ca.astype(BF).astype(F32)
            low = ca - high
            for dst, val in ((highs, high), (lows, low)):
                dst.append(
                    jnp.concatenate(
                        [jnp.where(sub == lane // 32 + 4 * h, val, 0.0) for h in range(2)], axis=1
                    )
                )
        lhs = jnp.concatenate(highs + lows, axis=0).astype(BF)
        total = jnp.zeros((8, 128), F32)
        for yb in range(TH // 8):
            block = dbuf[yb * 256 : (yb + 1) * 256, v * TW : (v + 1) * TW]
            o = jnp.dot(lhs, block, preferred_element_type=F32)
            o = o[:24] + o[24:]
            model = o[0:8] + col_coord * o[8:16] + (row_coord + yb / 8.0) * o[16:24]
            rows8 = pl.ds(yb * 8, 8)
            diff = visits[v, rows8, :] - model
            diff_out[v, rows8, :] = diff
            total = total + visits[V + v, rows8, :] * (diff * diff)
        tot_rows.append(jnp.sum(total, axis=0, keepdims=True))
    tot_rows += [jnp.zeros((1, 128), F32)] * 4
    tot_out[...] = jnp.broadcast_to(
        jnp.sum(jnp.concatenate(tot_rows, axis=0), axis=1, keepdims=True), (8, 128)
    )


def table_array():
    table = kernel_table()
    tables = np.zeros((512, F * TW), BF)
    tables[0:256] = column_matrix(table)
    rows = row_matrix(table)
    tables[256:512, 0:KDIM] = rows[0:256]
    tables[256:512, 640 : 640 + KDIM] = rows[256:512]
    return jnp.asarray(tables)


VMEM = pl.BlockSpec(memory_space=pltpu.VMEM)
SMEM = pl.BlockSpec(memory_space=pltpu.SMEM)
PARAMS = pltpu.CompilerParams(vmem_limit_bytes=16 * 1024 * 1024)


def basis_kernel(dither, parity, mid, side_a, side_b, visits):
    return pl.pallas_call(
        basis_body,
        out_shape=jax.ShapeDtypeStruct((TH * 32, V * TW), BF),
        in_specs=[SMEM] * 2 + [VMEM] * 5,
        out_specs=VMEM,
        scratch_shapes=[
            pltpu.VMEM((3, PROWS, 128), F32),
            pltpu.VMEM((F, WROWS, V * TW), BF),
            pltpu.VMEM((TH, V * TW), BF),
        ],
        compiler_params=PARAMS,
        name="basis",
    )(dither, parity, mid, side_a, side_b, visits, table_array())


def fit_kernel(dither, stamps, parity, mid, side_a, side_b, visits, basis):
    return pl.pallas_call(
        fit_body,
        out_shape=(
            jax.ShapeDtypeStruct((V, TH, TW), F32),
            jax.ShapeDtypeStruct((V, TH, TW), F32),
            jax.ShapeDtypeStruct((8, 128), F32),
        ),
        in_specs=[SMEM] * 3 + [VMEM] * 5,
        out_specs=(VMEM, VMEM, VMEM),
        scratch_shapes=[
            pltpu.VMEM((3, PROWS, 128), F32),
            pltpu.VMEM((V, 4, 32, 128), F32),
            pltpu.VMEM((V, TH, TW), F32),
        ],
        compiler_params=PARAMS,
        name="fit",
    )(dither, stamps, parity, mid, side_a, side_b, visits, basis)


def exchange(x, axis, first):
    pairs = []
    for i in range(first, lax.axis_size(axis) - 1, 2):
        pairs += [(i, i + 1), (i + 1, i)]
    return lax.ppermute(x, axis, pairs)


def strip_sum(x):
    count = lax.axis_size("fcol")
    parts = jnp.broadcast_to(x[None, :], (count, x.shape[0]))
    return jnp.sum(lax.all_to_all(parts, "fcol", 0, 0, tiled=True), axis=0)


def on_device(science, pixel_mask, coadd_image, coadd_variance, dither, stamps):
    parity = jnp.bitwise_and(jnp.stack([lax.axis_index("frow"), lax.axis_index("fcol")]), 1)
    planes = lax.optimization_barrier(jnp.stack([coadd_image, coadd_variance]))
    rows_a = exchange(planes, "frow", 1)
    rows_b = exchange(planes, "frow", 0)
    mid = jnp.concatenate([rows_a, planes, rows_b], axis=1)
    mid, science, pixel_mask = lax.optimization_barrier((mid, science, pixel_mask))
    visits = jnp.concatenate([science, (pixel_mask == 0).astype(F32)], axis=0)
    image_a = exchange(mid[0], "fcol", 1)
    side_b = exchange(mid, "fcol", 0)
    var_a = exchange(mid[1], "fcol", 1)
    basis = basis_kernel(dither, parity, mid, image_a, side_b, visits)
    diff, var, tot = fit_kernel(
        dither, stamps.reshape(V, SMAX), parity, mid, var_a, side_b, visits, basis
    )
    tot = strip_sum(tot[:V, 0])
    pixel_count = TH * TW * lax.axis_size("fcol")
    noise = tot.reshape(V, 1, 1) / pixel_count
    return diff * lax.rsqrt(noise + var + 1e-06)


def solution(mesh):
    in_specs = (
        P(None, "frow", "fcol"),
        P(None, "frow", "fcol"),
        P("frow", "fcol"),
        P("frow", "fcol"),
        P(),
        P(None, "frow", "fcol", None),
    )
    out_specs = P(None, "frow", "fcol")
    return jax.shard_map(
        on_device, mesh=mesh, in_specs=in_specs, out_specs=out_specs, check_vma=False
    )
```

```python
import functools

import jax
import jax.numpy as jnp
import numpy as np
from jax import lax
from jax.experimental import pallas as pl
from jax.experimental.pallas import tpu as pltpu
from jax.sharding import PartitionSpec as P

V = 4
TH = 128
TW = 128
R = 15
NB = 30
STAMP = 32
DMAX = 113
SMAX = 12
SPREADS = (0.75, 1.5, 3.0)
MARGIN = DMAX + R
F = 12
WROWS = 160
SLAB = 48
YB = 16
KDIM = F * SLAB + 2 * YB
PROWS = 392
BF = jnp.bfloat16
F32 = jnp.float32


def kernel_table():
    offsets = np.arange(-R, R + 1, dtype=np.float32)
    profiles = []
    for spread in SPREADS:
        for degree in range(4):
            profile = np.exp(-offsets * offsets / np.float32(2.0 * spread * spread)) * (
                offsets / np.float32(spread)
            ) ** degree
            profile = profile.astype(np.float32)
            profiles.append(profile / np.sqrt(np.sum(profile * profile)))
    return np.stack(profiles).astype(BF)


def basis_pairs():
    pairs = []
    for g in range(3):
        for a in range(4):
            for b in range(4 - a):
                pairs.append((4 * g + a, 4 * g + b))
    return pairs


def column_matrix(table):
    out = np.zeros((256, F * TW), BF)
    for f in range(F):
        for x in range(TW):
            out[x : x + 2 * R + 1, f * TW + x] = table[f]
    return out


def row_matrix(table):
    out = np.zeros((YB * 32, KDIM), BF)
    for k, (r, c) in enumerate(basis_pairs()):
        for y in range(YB):
            out[y * 32 + k, c * SLAB + y : c * SLAB + y + 2 * R + 1] = table[r]
    for y in range(YB):
        out[y * 32 + NB, F * SLAB + YB] = 1.0
        out[y * 32 + NB + 1, F * SLAB + y] = 1.0
    return out


def roll_lanes(x, shift):
    return pltpu.roll(x, shift, 1)


def gather_planes(planes, parity, mid, side_a, side_b):
    row_a = pl.multiple_of(parity[0] * 256, 128)
    row_b = pl.multiple_of(256 - parity[0] * 256, 128)
    for b, ref in ((1, mid), (2 * parity[1], side_a), (2 - 2 * parity[1], side_b)):
        planes[b, pl.ds(row_a, 128), :] = ref[0:128, :]
        planes[b, 128:256, :] = ref[128:256, :]
        planes[b, pl.ds(row_b, 128), :] = ref[256:384, :]
        planes[b, 384:PROWS, :] = jnp.zeros((PROWS - 384, 128), F32)


def basis_body(dither, parity, mid, side_a, side_b, visits, tables, dbuf, planes, cbuf, sbuf):
    gather_planes(planes, parity, mid.at[0], side_a, side_b.at[0])
    lane1 = lax.broadcasted_iota(jnp.int32, (1, 128), 1)
    windows = []
    for v in range(V):
        row0 = DMAX + dither[v, 0]
        col0 = DMAX + dither[v, 1]
        b0 = lax.shift_right_logical(col0, 7)
        s = jnp.bitwise_and(col0, 127)
        back = jnp.bitwise_and(128 - s, 127)
        last = jnp.minimum(b0 + 2, 2)
        t0 = roll_lanes(planes[b0, pl.ds(row0, WROWS), :], back)
        t1 = roll_lanes(planes[b0 + 1, pl.ds(row0, WROWS), :], back)
        t2 = roll_lanes(planes[last, pl.ds(row0, WROWS), :], back)
        keep = lane1 < 128 - s
        windows.append(
            jnp.concatenate([jnp.where(keep, t0, t1), jnp.where(keep, t1, t2)], axis=1).astype(BF)
        )
        sbuf[:, v * TW : (v + 1) * TW] = visits[v].astype(BF)

    for v in range(V):
        cp = jnp.dot(windows[v], tables[0:256, :], preferred_element_type=F32).astype(BF)
        for f in range(F):
            cbuf[f, :, v * TW : (v + 1) * TW] = cp[:, f * TW : (f + 1) * TW]

    ones_piece = jnp.ones((YB, V * TW), BF)

    def row_block(yb, carry):
        base = pl.multiple_of(yb * YB, YB)
        slab = jnp.concatenate(
            [cbuf[f, pl.ds(base, SLAB), :] for f in range(F)]
            + [sbuf[pl.ds(base, YB), :], ones_piece],
            axis=0,
        )
        trow = jnp.concatenate([tables[256:512, 0:KDIM], tables[256:512, 640 : 640 + KDIM]], axis=0)
        out = jnp.dot(trow, slab, preferred_element_type=F32).astype(BF)
        dbuf[pl.ds(pl.multiple_of(yb * (YB * 32), YB * 32), YB * 32), :] = out
        return carry

    lax.fori_loop(0, TH // YB, row_block, 0, unroll=2)


def fit_body(dither, stamps, parity, mid, side_a, side_b, visits, dbuf,
             diff_out, var_out, tot_out, planes, gbuf, wbuf):
    gather_planes(planes, parity, mid.at[1], side_a, side_b.at[1])
    lane = lax.broadcasted_iota(jnp.int32, (8, 128), 1)
    sub = lax.broadcasted_iota(jnp.int32, (8, 128), 0)
    lane1 = lane[0:1]
    for v in range(V):
        row1 = MARGIN + dither[v, 0]
        col1 = MARGIN + dither[v, 1]
        b1 = lax.shift_right_logical(col1, 7)
        s1 = jnp.bitwise_and(col1, 127)
        back1 = jnp.bitwise_and(128 - s1, 127)
        nxt = jnp.minimum(b1 + 1, 2)
        q0 = roll_lanes(planes[b1, pl.ds(row1, TH), :], back1)
        q1 = roll_lanes(planes[nxt, pl.ds(row1, TH), :], back1)
        var = jnp.where(lane1 < 128 - s1, q0, q1)
        var_out[v] = var
        wbuf[v] = visits[V + v] / (0.25 + var)

    lanes32 = lax.broadcasted_iota(jnp.int32, (32, 128), 1)
    half_masks = [(lanes32 // 64 == h).astype(F32) for h in range(2)]
    odd_masks = [((lanes32 // 32) % 2 == h).astype(F32).astype(BF) for h in range(2)]
    for v in range(V):

        def gram_row(i, carry, v=v):
            acc = jnp.zeros((64, 64), F32)
            for c in range(8):
                ws = []
                ds = []
                for t in range(4):
                    y = i * 32 + c * 4 + t
                    d = dbuf[pl.ds(pl.multiple_of(y * 32, 32), 32), v * TW : (v + 1) * TW]
                    w = d.astype(F32) * wbuf[v, pl.ds(y, 1), :]
                    ws.append(jnp.concatenate([(w * m).astype(BF) for m in half_masks], axis=0))
                    ds.append(jnp.concatenate([d * m for m in odd_masks], axis=0))
                acc = acc + lax.dot_general(
                    jnp.concatenate(ws, axis=1),
                    jnp.concatenate(ds, axis=1),
                    (((1,), (1,)), ((), ())),
                    preferred_element_type=F32,
                )
            gbuf[v, i] = jnp.concatenate([acc[:32], acc[32:]], axis=1)
            return carry

        lax.fori_loop(0, 4, gram_row, 0, unroll=2)

    group = lane // 32
    xs = (group.astype(F32) - 1.5) * 0.5
    mats = []
    for v in range(V):
        use = jnp.zeros((8, 128), F32)
        cell = sub * 4 + group
        for s in range(SMAX):
            use = use + (cell == stamps[v, s]).astype(F32)
        m00 = jnp.zeros((32, 128), F32)
        m02 = jnp.zeros((32, 128), F32)
        m22 = jnp.zeros((32, 128), F32)
        for i in range(4):
            h = gbuf[v, i] * use[i : i + 1, :]
            ys = (i - 1.5) * 0.5
            m00 = m00 + h
            m02 = m02 + h * ys
            m22 = m22 + h * (ys * ys)
        x1 = xs[0:1]

        def fold(m):
            m = m + roll_lanes(m, 32)
            return m + roll_lanes(m, 64)

        m01 = fold(m00 * x1)
        m11 = fold(m00 * (x1 * x1))
        m12 = fold(m02 * x1)
        m00 = fold(m00)
        m02 = fold(m02)
        m22 = fold(m22)
        g1 = lane1 // 32
        zero = jnp.zeros((32, 128), F32)

        def block_row(a, b, c):
            return jnp.where(g1 == 0, a, jnp.where(g1 == 1, b, jnp.where(g1 == 2, c, zero)))

        mat = jnp.concatenate(
            [
                block_row(m00, m01, m02),
                block_row(m01, m11, m12),
                block_row(m02, m12, m22),
                zero,
            ],
            axis=0,
        )
        rows = lax.broadcasted_iota(jnp.int32, (128, 128), 0)
        cols = lax.broadcasted_iota(jnp.int32, (128, 128), 1)
        valid_col = (cols % 32) != 31
        mat = jnp.where(valid_col & ((rows % 32) != 31), 0.5 * (mat + mat.T), mat)
        diag = (rows == cols) & valid_col & (rows < 96)
        trace = jnp.sum(jnp.where(diag, mat, 0.0), keepdims=True)
        mat = jnp.where(diag, mat + 0.001 * trace / 93.0, mat)
        mats.append([mat[8 * r : 8 * r + 8] for r in range(12)])

    def lane_of(x, p):
        return jnp.broadcast_to(x[:, p : p + 1], (8, 128))

    for a in range(3):
        block = [[mats[v][4 * a + q] for q in range(4)] for v in range(V)]
        for q in range(4):
            pivots = [i for i in range(8) if 8 * q + i != 31]
            lanes = {i: 32 * a + 8 * q + i for i in pivots}
            cols = [{} for _ in range(V)]
            others = [{} for _ in range(V)]
            for i in pivots:
                for v in range(V):
                    cols[v][i] = lane_of(block[v][q], lanes[i])
            for i in pivots:
                for o in range(4):
                    if o != q:
                        for v in range(V):
                            others[v][o, i] = lane_of(block[v][o], lanes[i])
            for i in pivots:
                for v in range(V):
                    col = cols[v][i]
                    inv = 1.0 / col[i : i + 1]
                    mult = jnp.where(sub == i, -1.0, col)

                    def step(x):
                        return jnp.where(sub == i, 0.0, x) - mult * (x[i : i + 1] * inv)

                    block[v][q] = step(block[v][q])
                    for j in pivots:
                        if j > i:
                            cols[v][j] = step(cols[v][j])
            for v in range(V):
                for o in range(4):
                    if o != q:
                        acc = block[v][o]
                        for i in pivots:
                            acc = acc - others[v][o, i] * block[v][q][i : i + 1]
                        block[v][o] = acc
        rest = [r for r in range(12) if r // 4 != a]
        for v in range(V):
            for q in range(4):
                mats[v][4 * a + q] = block[v][q]
            solved = jnp.concatenate(block[v][:3] + [jnp.where(sub == 7, 0.0, block[v][3])], axis=0)
            zero = jnp.zeros((32, 128), F32)
            factor = jnp.concatenate([solved if t == a else zero for t in range(4)], axis=0)
            old = jnp.concatenate([mats[v][r] for r in rest], axis=0)
            upd = old - jnp.dot(old, factor, preferred_element_type=F32, precision=lax.Precision.HIGHEST)
            for n, r in enumerate(rest):
                mats[v][r] = upd[8 * n : 8 * n + 8]

    row_coord = (lax.broadcasted_iota(jnp.int32, (8, 128), 0).astype(F32) + 0.5 - 64.0) / 64.0
    col_coord = (lane.astype(F32) + 0.5 - 64.0) / 64.0
    tot_rows = []
    for v in range(V):
        vec = jnp.zeros((8, 128), F32)
        for b in range(12):
            colb = jnp.broadcast_to(mats[v][b][:, 31:32], (8, 128))
            vec = vec + jnp.where(lane == sub + 8 * b, colb, 0.0)
        vec = jnp.sum(vec, axis=0, keepdims=True)
        highs = []
        lows = []
        for a in range(3):
            ca = jnp.broadcast_to(jnp.where(lane1 // 32 == a, vec, 0.0), (8, 128))
            ca = ca + roll_lanes(ca, 32)
            ca = ca + roll_lanes(ca, 64)
            ca = jnp.where(lane % 32 == 31, 0.0, ca)
            high = ca.astype(BF).astype(F32)
            low = ca - high
            for dst, val in ((highs, high), (lows, low)):
                dst.append(
                    jnp.concatenate(
                        [jnp.where(sub == lane // 32 + 4 * h, val, 0.0) for h in range(2)], axis=1
                    )
                )
        lhs = jnp.concatenate(highs + lows, axis=0).astype(BF)
        total = jnp.zeros((8, 128), F32)
        for yb in range(TH // 8):
            block = dbuf[yb * 256 : (yb + 1) * 256, v * TW : (v + 1) * TW]
            o = jnp.dot(lhs, block, preferred_element_type=F32)
            o = o[:24] + o[24:]
            model = o[0:8] + col_coord * o[8:16] + (row_coord + yb / 8.0) * o[16:24]
            rows8 = pl.ds(yb * 8, 8)
            diff = visits[v, rows8, :] - model
            diff_out[v, rows8, :] = diff
            total = total + visits[V + v, rows8, :] * (diff * diff)
        tot_rows.append(jnp.sum(total, axis=0, keepdims=True))
    tot_rows += [jnp.zeros((1, 128), F32)] * 4
    tot_out[...] = jnp.broadcast_to(
        jnp.sum(jnp.concatenate(tot_rows, axis=0), axis=1, keepdims=True), (8, 128)
    )


def table_array():
    table = kernel_table()
    tables = np.zeros((512, F * TW), BF)
    tables[0:256] = column_matrix(table)
    rows = row_matrix(table)
    tables[256:512, 0:KDIM] = rows[0:256]
    tables[256:512, 640 : 640 + KDIM] = rows[256:512]
    return jnp.asarray(tables)


VMEM = pl.BlockSpec(memory_space=pltpu.VMEM)
SMEM = pl.BlockSpec(memory_space=pltpu.SMEM)
PARAMS = pltpu.CompilerParams(vmem_limit_bytes=16 * 1024 * 1024)


def basis_kernel(dither, parity, mid, side_a, side_b, visits):
    return pl.pallas_call(
        basis_body,
        out_shape=jax.ShapeDtypeStruct((TH * 32, V * TW), BF),
        in_specs=[SMEM] * 2 + [VMEM] * 5,
        out_specs=VMEM,
        scratch_shapes=[
            pltpu.VMEM((3, PROWS, 128), F32),
            pltpu.VMEM((F, WROWS, V * TW), BF),
            pltpu.VMEM((TH, V * TW), BF),
        ],
        compiler_params=PARAMS,
        name="basis",
    )(dither, parity, mid, side_a, side_b, visits, table_array())


def fit_kernel(dither, stamps, parity, mid, side_a, side_b, visits, basis):
    return pl.pallas_call(
        fit_body,
        out_shape=(
            jax.ShapeDtypeStruct((V, TH, TW), F32),
            jax.ShapeDtypeStruct((V, TH, TW), F32),
            jax.ShapeDtypeStruct((8, 128), F32),
        ),
        in_specs=[SMEM] * 3 + [VMEM] * 5,
        out_specs=(VMEM, VMEM, VMEM),
        scratch_shapes=[
            pltpu.VMEM((3, PROWS, 128), F32),
            pltpu.VMEM((V, 4, 32, 128), F32),
            pltpu.VMEM((V, TH, TW), F32),
        ],
        compiler_params=PARAMS,
        name="fit",
    )(dither, stamps, parity, mid, side_a, side_b, visits, basis)


def exchange(x, axis, first):
    pairs = []
    for i in range(first, lax.axis_size(axis) - 1, 2):
        pairs += [(i, i + 1), (i + 1, i)]
    return lax.ppermute(x, axis, pairs)


def strip_sum(x):
    count = lax.axis_size("fcol")
    parts = jnp.broadcast_to(x[None, :], (count, x.shape[0]))
    return jnp.sum(lax.all_to_all(parts, "fcol", 0, 0, tiled=True), axis=0)


def on_device(science, pixel_mask, coadd_image, coadd_variance, dither, stamps):
    parity = jnp.bitwise_and(jnp.stack([lax.axis_index("frow"), lax.axis_index("fcol")]), 1)
    planes = lax.optimization_barrier(jnp.stack([coadd_image, coadd_variance]))
    rows_a = exchange(planes, "frow", 1)
    rows_b = exchange(planes, "frow", 0)
    mid = jnp.concatenate([rows_a, planes, rows_b], axis=1)
    mid, science, pixel_mask = lax.optimization_barrier((mid, science, pixel_mask))
    visits = jnp.concatenate([science, (pixel_mask == 0).astype(F32)], axis=0)
    image_a = exchange(mid[0], "fcol", 1)
    side_b = exchange(mid, "fcol", 0)
    var_a = exchange(mid[1], "fcol", 1)
    basis = basis_kernel(dither, parity, mid, image_a, side_b, visits)
    diff, var, tot = fit_kernel(
        dither, stamps.reshape(V, SMAX), parity, mid, var_a, side_b, visits, basis
    )
    tot = strip_sum(tot[:V, 0])
    pixel_count = TH * TW * lax.axis_size("fcol")
    noise = tot.reshape(V, 1, 1) / pixel_count
    return diff * lax.rsqrt(noise + var + 1e-06)


def solution(mesh):
    in_specs = (
        P(None, "frow", "fcol"),
        P(None, "frow", "fcol"),
        P("frow", "fcol"),
        P("frow", "fcol"),
        P(),
        P(None, "frow", "fcol", None),
    )
    out_specs = P(None, "frow", "fcol")
    return jax.shard_map(
        on_device, mesh=mesh, in_specs=in_specs, out_specs=out_specs, check_vma=False
    )
```

```python
import functools

import jax
import jax.numpy as jnp
import numpy as np
from jax import lax
from jax.experimental import pallas as pl
from jax.experimental.pallas import tpu as pltpu
from jax.sharding import PartitionSpec as P

V = 4
TH = 128
TW = 128
R = 15
NB = 30
STAMP = 32
DMAX = 113
SMAX = 12
SPREADS = (0.75, 1.5, 3.0)
MARGIN = DMAX + R
F = 12
WROWS = 160
SLAB = 48
YB = 16
KDIM = F * SLAB + 2 * YB
PROWS = 392
BF = jnp.bfloat16
F32 = jnp.float32


def kernel_table():
    offsets = np.arange(-R, R + 1, dtype=np.float32)
    profiles = []
    for spread in SPREADS:
        for degree in range(4):
            profile = np.exp(-offsets * offsets / np.float32(2.0 * spread * spread)) * (
                offsets / np.float32(spread)
            ) ** degree
            profile = profile.astype(np.float32)
            profiles.append(profile / np.sqrt(np.sum(profile * profile)))
    return np.stack(profiles).astype(BF)


def basis_pairs():
    pairs = []
    for g in range(3):
        for a in range(4):
            for b in range(4 - a):
                pairs.append((4 * g + a, 4 * g + b))
    return pairs


def column_matrix(table):
    out = np.zeros((256, F * TW), BF)
    for f in range(F):
        for x in range(TW):
            out[x : x + 2 * R + 1, f * TW + x] = table[f]
    return out


def row_matrix(table):
    out = np.zeros((YB * 32, KDIM), BF)
    for k, (r, c) in enumerate(basis_pairs()):
        for y in range(YB):
            out[y * 32 + k, c * SLAB + y : c * SLAB + y + 2 * R + 1] = table[r]
    for y in range(YB):
        out[y * 32 + NB, F * SLAB + YB] = 1.0
        out[y * 32 + NB + 1, F * SLAB + y] = 1.0
    return out


def roll_lanes(x, shift):
    return pltpu.roll(x, shift, 1)


def gather_planes(planes, parity, mid, side_a, side_b):
    row_a = pl.multiple_of(parity[0] * 256, 128)
    row_b = pl.multiple_of(256 - parity[0] * 256, 128)
    for b, ref in ((1, mid), (2 * parity[1], side_a), (2 - 2 * parity[1], side_b)):
        planes[b, pl.ds(row_a, 128), :] = ref[0:128, :]
        planes[b, 128:256, :] = ref[128:256, :]
        planes[b, pl.ds(row_b, 128), :] = ref[256:384, :]
        planes[b, 384:PROWS, :] = jnp.zeros((PROWS - 384, 128), F32)


def basis_body(dither, parity, mid, side_a, side_b, visits, tables, dbuf, planes, cbuf, sbuf):
    gather_planes(planes, parity, mid.at[0], side_a, side_b.at[0])
    lane1 = lax.broadcasted_iota(jnp.int32, (1, 128), 1)
    windows = []
    for v in range(V):
        row0 = DMAX + dither[v, 0]
        col0 = DMAX + dither[v, 1]
        b0 = lax.shift_right_logical(col0, 7)
        s = jnp.bitwise_and(col0, 127)
        back = jnp.bitwise_and(128 - s, 127)
        last = jnp.minimum(b0 + 2, 2)
        t0 = roll_lanes(planes[b0, pl.ds(row0, WROWS), :], back)
        t1 = roll_lanes(planes[b0 + 1, pl.ds(row0, WROWS), :], back)
        t2 = roll_lanes(planes[last, pl.ds(row0, WROWS), :], back)
        keep = lane1 < 128 - s
        windows.append(
            jnp.concatenate([jnp.where(keep, t0, t1), jnp.where(keep, t1, t2)], axis=1).astype(BF)
        )
        sbuf[:, v * TW : (v + 1) * TW] = visits[v].astype(BF)

    for v in range(V):
        cp = jnp.dot(windows[v], tables[0:256, :], preferred_element_type=F32).astype(BF)
        for f in range(F):
            cbuf[f, :, v * TW : (v + 1) * TW] = cp[:, f * TW : (f + 1) * TW]

    ones_piece = jnp.ones((YB, V * TW), BF)

    def row_block(yb, carry):
        base = pl.multiple_of(yb * YB, YB)
        slab = jnp.concatenate(
            [cbuf[f, pl.ds(base, SLAB), :] for f in range(F)]
            + [sbuf[pl.ds(base, YB), :], ones_piece],
            axis=0,
        )
        trow = jnp.concatenate([tables[256:512, 0:KDIM], tables[256:512, 640 : 640 + KDIM]], axis=0)
        out = jnp.dot(trow, slab, preferred_element_type=F32).astype(BF)
        dbuf[pl.ds(pl.multiple_of(yb * (YB * 32), YB * 32), YB * 32), :] = out
        return carry

    lax.fori_loop(0, TH // YB, row_block, 0, unroll=4)


def fit_body(dither, stamps, parity, mid, side_a, side_b, visits, dbuf,
             diff_out, var_out, tot_out, planes, gbuf, wbuf):
    gather_planes(planes, parity, mid.at[1], side_a, side_b.at[1])
    lane = lax.broadcasted_iota(jnp.int32, (8, 128), 1)
    sub = lax.broadcasted_iota(jnp.int32, (8, 128), 0)
    lane1 = lane[0:1]
    for v in range(V):
        row1 = MARGIN + dither[v, 0]
        col1 = MARGIN + dither[v, 1]
        b1 = lax.shift_right_logical(col1, 7)
        s1 = jnp.bitwise_and(col1, 127)
        back1 = jnp.bitwise_and(128 - s1, 127)
        nxt = jnp.minimum(b1 + 1, 2)
        q0 = roll_lanes(planes[b1, pl.ds(row1, TH), :], back1)
        q1 = roll_lanes(planes[nxt, pl.ds(row1, TH), :], back1)
        var = jnp.where(lane1 < 128 - s1, q0, q1)
        var_out[v] = var
        wbuf[v] = visits[V + v] / (0.25 + var)

    lanes32 = lax.broadcasted_iota(jnp.int32, (32, 128), 1)
    half_masks = [(lanes32 // 64 == h).astype(F32) for h in range(2)]
    odd_masks = [((lanes32 // 32) % 2 == h).astype(F32).astype(BF) for h in range(2)]
    for v in range(V):

        def gram_row(i, carry, v=v):
            acc = jnp.zeros((64, 64), F32)
            for c in range(8):
                ws = []
                ds = []
                for t in range(4):
                    y = i * 32 + c * 4 + t
                    d = dbuf[pl.ds(pl.multiple_of(y * 32, 32), 32), v * TW : (v + 1) * TW]
                    w = d.astype(F32) * wbuf[v, pl.ds(y, 1), :]
                    ws.append(jnp.concatenate([(w * m).astype(BF) for m in half_masks], axis=0))
                    ds.append(jnp.concatenate([d * m for m in odd_masks], axis=0))
                acc = acc + lax.dot_general(
                    jnp.concatenate(ws, axis=1),
                    jnp.concatenate(ds, axis=1),
                    (((1,), (1,)), ((), ())),
                    preferred_element_type=F32,
                )
            gbuf[v, i] = jnp.concatenate([acc[:32], acc[32:]], axis=1)
            return carry

        lax.fori_loop(0, 4, gram_row, 0, unroll=4)

    group = lane // 32
    xs = (group.astype(F32) - 1.5) * 0.5
    mats = []
    for v in range(V):
        use = jnp.zeros((8, 128), F32)
        cell = sub * 4 + group
        for s in range(SMAX):
            use = use + (cell == stamps[v, s]).astype(F32)
        m00 = jnp.zeros((32, 128), F32)
        m02 = jnp.zeros((32, 128), F32)
        m22 = jnp.zeros((32, 128), F32)
        for i in range(4):
            h = gbuf[v, i] * use[i : i + 1, :]
            ys = (i - 1.5) * 0.5
            m00 = m00 + h
            m02 = m02 + h * ys
            m22 = m22 + h * (ys * ys)
        x1 = xs[0:1]

        def fold(m):
            m = m + roll_lanes(m, 32)
            return m + roll_lanes(m, 64)

        m01 = fold(m00 * x1)
        m11 = fold(m00 * (x1 * x1))
        m12 = fold(m02 * x1)
        m00 = fold(m00)
        m02 = fold(m02)
        m22 = fold(m22)
        g1 = lane1 // 32
        zero = jnp.zeros((32, 128), F32)

        def block_row(a, b, c):
            return jnp.where(g1 == 0, a, jnp.where(g1 == 1, b, jnp.where(g1 == 2, c, zero)))

        mat = jnp.concatenate(
            [
                block_row(m00, m01, m02),
                block_row(m01, m11, m12),
                block_row(m02, m12, m22),
                zero,
            ],
            axis=0,
        )
        rows = lax.broadcasted_iota(jnp.int32, (128, 128), 0)
        cols = lax.broadcasted_iota(jnp.int32, (128, 128), 1)
        valid_col = (cols % 32) != 31
        mat = jnp.where(valid_col & ((rows % 32) != 31), 0.5 * (mat + mat.T), mat)
        diag = (rows == cols) & valid_col & (rows < 96)
        trace = jnp.sum(jnp.where(diag, mat, 0.0), keepdims=True)
        mat = jnp.where(diag, mat + 0.001 * trace / 93.0, mat)
        mats.append([mat[8 * r : 8 * r + 8] for r in range(12)])

    def lane_of(x, p):
        return jnp.broadcast_to(x[:, p : p + 1], (8, 128))

    for a in range(3):
        block = [[mats[v][4 * a + q] for q in range(4)] for v in range(V)]
        for q in range(4):
            pivots = [i for i in range(8) if 8 * q + i != 31]
            lanes = {i: 32 * a + 8 * q + i for i in pivots}
            cols = [{} for _ in range(V)]
            others = [{} for _ in range(V)]
            for i in pivots:
                for v in range(V):
                    cols[v][i] = lane_of(block[v][q], lanes[i])
            for i in pivots:
                for o in range(4):
                    if o != q:
                        for v in range(V):
                            others[v][o, i] = lane_of(block[v][o], lanes[i])
            for i in pivots:
                for v in range(V):
                    col = cols[v][i]
                    inv = 1.0 / col[i : i + 1]
                    mult = jnp.where(sub == i, -1.0, col)

                    def step(x):
                        return jnp.where(sub == i, 0.0, x) - mult * (x[i : i + 1] * inv)

                    block[v][q] = step(block[v][q])
                    for j in pivots:
                        if j > i:
                            cols[v][j] = step(cols[v][j])
            for v in range(V):
                for o in range(4):
                    if o != q:
                        acc = block[v][o]
                        for i in pivots:
                            acc = acc - others[v][o, i] * block[v][q][i : i + 1]
                        block[v][o] = acc
        rest = [r for r in range(12) if r // 4 != a]
        for v in range(V):
            for q in range(4):
                mats[v][4 * a + q] = block[v][q]
            solved = jnp.concatenate(block[v][:3] + [jnp.where(sub == 7, 0.0, block[v][3])], axis=0)
            zero = jnp.zeros((32, 128), F32)
            factor = jnp.concatenate([solved if t == a else zero for t in range(4)], axis=0)
            old = jnp.concatenate([mats[v][r] for r in rest], axis=0)
            upd = old - jnp.dot(old, factor, preferred_element_type=F32, precision=lax.Precision.HIGHEST)
            for n, r in enumerate(rest):
                mats[v][r] = upd[8 * n : 8 * n + 8]

    row_coord = (lax.broadcasted_iota(jnp.int32, (8, 128), 0).astype(F32) + 0.5 - 64.0) / 64.0
    col_coord = (lane.astype(F32) + 0.5 - 64.0) / 64.0
    tot_rows = []
    for v in range(V):
        vec = jnp.zeros((8, 128), F32)
        for b in range(12):
            colb = jnp.broadcast_to(mats[v][b][:, 31:32], (8, 128))
            vec = vec + jnp.where(lane == sub + 8 * b, colb, 0.0)
        vec = jnp.sum(vec, axis=0, keepdims=True)
        highs = []
        lows = []
        for a in range(3):
            ca = jnp.broadcast_to(jnp.where(lane1 // 32 == a, vec, 0.0), (8, 128))
            ca = ca + roll_lanes(ca, 32)
            ca = ca + roll_lanes(ca, 64)
            ca = jnp.where(lane % 32 == 31, 0.0, ca)
            high = ca.astype(BF).astype(F32)
            low = ca - high
            for dst, val in ((highs, high), (lows, low)):
                dst.append(
                    jnp.concatenate(
                        [jnp.where(sub == lane // 32 + 4 * h, val, 0.0) for h in range(2)], axis=1
                    )
                )
        lhs = jnp.concatenate(highs + lows, axis=0).astype(BF)
        total = jnp.zeros((8, 128), F32)
        for yb in range(TH // 8):
            block = dbuf[yb * 256 : (yb + 1) * 256, v * TW : (v + 1) * TW]
            o = jnp.dot(lhs, block, preferred_element_type=F32)
            o = o[:24] + o[24:]
            model = o[0:8] + col_coord * o[8:16] + (row_coord + yb / 8.0) * o[16:24]
            rows8 = pl.ds(yb * 8, 8)
            diff = visits[v, rows8, :] - model
            diff_out[v, rows8, :] = diff
            total = total + visits[V + v, rows8, :] * (diff * diff)
        tot_rows.append(jnp.sum(total, axis=0, keepdims=True))
    tot_rows += [jnp.zeros((1, 128), F32)] * 4
    tot_out[...] = jnp.broadcast_to(
        jnp.sum(jnp.concatenate(tot_rows, axis=0), axis=1, keepdims=True), (8, 128)
    )


def table_array():
    table = kernel_table()
    tables = np.zeros((512, F * TW), BF)
    tables[0:256] = column_matrix(table)
    rows = row_matrix(table)
    tables[256:512, 0:KDIM] = rows[0:256]
    tables[256:512, 640 : 640 + KDIM] = rows[256:512]
    return jnp.asarray(tables)


VMEM = pl.BlockSpec(memory_space=pltpu.VMEM)
SMEM = pl.BlockSpec(memory_space=pltpu.SMEM)
PARAMS = pltpu.CompilerParams(vmem_limit_bytes=16 * 1024 * 1024)


def basis_kernel(dither, parity, mid, side_a, side_b, visits):
    return pl.pallas_call(
        basis_body,
        out_shape=jax.ShapeDtypeStruct((TH * 32, V * TW), BF),
        in_specs=[SMEM] * 2 + [VMEM] * 5,
        out_specs=VMEM,
        scratch_shapes=[
            pltpu.VMEM((3, PROWS, 128), F32),
            pltpu.VMEM((F, WROWS, V * TW), BF),
            pltpu.VMEM((TH, V * TW), BF),
        ],
        compiler_params=PARAMS,
        name="basis",
    )(dither, parity, mid, side_a, side_b, visits, table_array())


def fit_kernel(dither, stamps, parity, mid, side_a, side_b, visits, basis):
    return pl.pallas_call(
        fit_body,
        out_shape=(
            jax.ShapeDtypeStruct((V, TH, TW), F32),
            jax.ShapeDtypeStruct((V, TH, TW), F32),
            jax.ShapeDtypeStruct((8, 128), F32),
        ),
        in_specs=[SMEM] * 3 + [VMEM] * 5,
        out_specs=(VMEM, VMEM, VMEM),
        scratch_shapes=[
            pltpu.VMEM((3, PROWS, 128), F32),
            pltpu.VMEM((V, 4, 32, 128), F32),
            pltpu.VMEM((V, TH, TW), F32),
        ],
        compiler_params=PARAMS,
        name="fit",
    )(dither, stamps, parity, mid, side_a, side_b, visits, basis)


def exchange(x, axis, first):
    pairs = []
    for i in range(first, lax.axis_size(axis) - 1, 2):
        pairs += [(i, i + 1), (i + 1, i)]
    return lax.ppermute(x, axis, pairs)


def strip_sum(x):
    count = lax.axis_size("fcol")
    parts = jnp.broadcast_to(x[None, :], (count, x.shape[0]))
    return jnp.sum(lax.all_to_all(parts, "fcol", 0, 0, tiled=True), axis=0)


def on_device(science, pixel_mask, coadd_image, coadd_variance, dither, stamps):
    parity = jnp.bitwise_and(jnp.stack([lax.axis_index("frow"), lax.axis_index("fcol")]), 1)
    planes = lax.optimization_barrier(jnp.stack([coadd_image, coadd_variance]))
    rows_a = exchange(planes, "frow", 1)
    rows_b = exchange(planes, "frow", 0)
    mid = jnp.concatenate([rows_a, planes, rows_b], axis=1)
    mid, science, pixel_mask = lax.optimization_barrier((mid, science, pixel_mask))
    visits = jnp.concatenate([science, (pixel_mask == 0).astype(F32)], axis=0)
    image_a = exchange(mid[0], "fcol", 1)
    side_b = exchange(mid, "fcol", 0)
    var_a = exchange(mid[1], "fcol", 1)
    basis = basis_kernel(dither, parity, mid, image_a, side_b, visits)
    diff, var, tot = fit_kernel(
        dither, stamps.reshape(V, SMAX), parity, mid, var_a, side_b, visits, basis
    )
    tot = strip_sum(tot[:V, 0])
    pixel_count = TH * TW * lax.axis_size("fcol")
    noise = tot.reshape(V, 1, 1) / pixel_count
    return diff * lax.rsqrt(noise + var + 1e-06)


def solution(mesh):
    in_specs = (
        P(None, "frow", "fcol"),
        P(None, "frow", "fcol"),
        P("frow", "fcol"),
        P("frow", "fcol"),
        P(),
        P(None, "frow", "fcol", None),
    )
    out_specs = P(None, "frow", "fcol")
    return jax.shard_map(
        on_device, mesh=mesh, in_specs=in_specs, out_specs=out_specs, check_vma=False
    )
```
